128 devices in a mesh: band: 16 (over y, z), grid: 8 (over x, core).
Axes of the slice: x: 4, y: 4, z: 4, core: 2. Of those that a mesh axis runs over, the one named last changes fastest.
Arguments:
- x_initial: float32 [640, 3, 256, 256], P(('band', 'grid')), may hold values from -0.1 to 1, as said below
- sp2_choices: int32 [4], replicated, may hold values from 0 to 1, as said below
- domain_blocks: int32 [384, 5], replicated, may hold values from -1 to 639, as said below
- basis_values: bfloat16 [384, 768, 1280], P(('band', 'grid')), may hold values from -0.25 to 0.25
Outputs:
- density: float32 [640, 3, 256, 256], P(('band', 'grid'))
- hamiltonian: float32 [640, 3, 256, 256], P(('band', 'grid'))
- potential: float32 [384, 768], P(('band', 'grid'))
The draws below stay inside these ranges and needn't reach their ends.
Inputs may be any that keep to these rules, and one draw needn't show every extreme that they name: Lower block form of a symmetric matrix: each x_initial[I, 2] is symmetric, and the blocks x_initial[I, q] with I - 2 + q < 0 are zero. `domain_blocks`: domain rows are grouped by device in the order of the joined axes band then grid, 3 rows a device. A row lists 2 to 5 consecutive block numbers followed by -1 entries. All blocks of a domain are block rows of one device with the same grid index whose band index differs from the domain's device by at most 2; the domains of one device lie on different devices. Every device has a domain of 5 blocks. `sp2_choices`: not all steps apply the same polynomial.
All inputs are finite; a program needn't handle non-finite values.
Results may differ from the reference program's by a relative error of at most 0.0017.
The reference program's roundings to bfloat16 on the way count: a program that leaves them out, or rounds other values in their place, can miss the bound.
Values may be sent and summed in bfloat16 or wider, within the bound.
No kernel may reach another device: no remote copies, remote signals or barrier semaphores. Data moves between devices by JAX's collectives and lax.ppermute only.
A program may use at most 128 MiB of HBM per device.

```python
import jax
import jax.numpy as jnp
from jax import lax

BS = 256
DBLK = 5
NPT = 768
RB = 5
DOM = 3
REACH = 2
ITERS = 4
DOMAINS = 384
N_BAND = 16
N_GRID = 8


def draw_sp2_choices(key, part):
    values = jax.random.randint(jax.random.fold_in(key, 7), (ITERS,), 0, 2).astype(jnp.int32)
    alike = jnp.all(values == values[0])
    last_value = jnp.where(alike, 1 - values[ITERS - 1], values[ITERS - 1]).astype(jnp.int32)
    return values.at[ITERS - 1].set(last_value).astype(jnp.int32)


def draw_x_initial(key, part):
    row_total = RB * N_BAND * N_GRID
    key_level, key_noise = jax.random.split(key)
    levels = jax.random.uniform(key_level, (row_total, BS), jnp.float32, 0.2, 0.8)
    noise_blocks = 0.004 * jax.random.normal(key_noise, (row_total, 3, BS, BS), jnp.float32)
    diagonal = 0.5 * (noise_blocks[:, 2] + jnp.swapaxes(noise_blocks[:, 2], 1, 2))
    identity_matrix = jnp.eye(BS, dtype=jnp.float32)
    diagonal = diagonal + levels[:, :, None] * identity_matrix[None]
    lower_blocks = jnp.concatenate([noise_blocks[:, :2], diagonal[:, None]], axis=1)
    row_index = jnp.arange(row_total, dtype=jnp.int32)[:, None]
    slot_index = jnp.arange(3, dtype=jnp.int32)[None, :]
    present = (row_index - 2 + slot_index >= 0).astype(jnp.float32)
    return lower_blocks * present[:, :, None, None]


def draw_domain_blocks(key, part):
    device_total = N_BAND * N_GRID
    slot_total = 2 * REACH + 1
    key_order, key_count, key_full, key_place = jax.random.split(key, 4)
    device_ids = jnp.arange(device_total, dtype=jnp.int32)
    band_ids = device_ids // N_GRID
    grid_ids = device_ids % N_GRID
    band_moves = jnp.arange(slot_total, dtype=jnp.int32) - REACH
    target_band = band_ids[:, None] + band_moves[None, :]
    allowed = (target_band >= 0) & (target_band < N_BAND)
    scores = jax.random.randint(key_order, (device_total, slot_total), 0, 1024) * 16 + jnp.arange(slot_total, dtype=jnp.int32)[None, :]
    scores = jnp.where(allowed, scores, 1 << 20)
    ranking = jnp.argsort(scores, axis=1, stable=True)[:, :DOM]
    chosen_band = jnp.take_along_axis(target_band, ranking, axis=1)
    owners = chosen_band * N_GRID + grid_ids[:, None]
    counts = jax.random.randint(key_count, (device_total, DOM), 2, DBLK + 1)
    full_slot = jax.random.randint(key_full, (device_total, 1), 0, DOM)
    counts = jnp.where(jnp.arange(DOM, dtype=jnp.int32)[None, :] == full_slot, DBLK, counts)
    offset_rows = jax.random.randint(key_place, (device_total, DOM), 0, 1 << 20) % (RB - counts + 1)
    first_block = owners * RB + offset_rows
    positions = jnp.arange(DBLK, dtype=jnp.int32)
    block_ids = jnp.where(positions[None, None, :] < counts[:, :, None], first_block[:, :, None] + positions[None, None, :], -1)
    return block_ids.reshape(device_total * DOM, DBLK).astype(jnp.int32)


def steps_of(key, extent, cuts, low, top_value):
    def one(position, blocks):
        draws = jax.random.uniform(jax.random.fold_in(jax.random.fold_in(key, 6), position), (blocks,), jnp.float32, low / len(cuts), top_value / len(cuts))
        return jnp.repeat(jnp.exp(draws), extent[position] // blocks).reshape((-1,) + (1,) * (len(extent) - position - 1))

    gain = one(*cuts[0])
    for cut in cuts[1:]:
        gain = gain * one(*cut)
    return gain


def bell_draw(stream_key, dims, deviation, reach, cuts=(), held_as=jnp.bfloat16):
    factor_of = steps_of(stream_key, dims, cuts, -0.22, 0.18) if cuts else 1.0
    drawn = jax.random.normal(stream_key, dims, jnp.float32) * deviation * factor_of
    return jnp.minimum(jnp.maximum(drawn, -reach), reach).astype(held_as)


def setup_inputs(seed: int = 0) -> dict:
    arg_keys = jax.random.split(jax.random.key(seed), 5)
    return {
        "x_initial": draw_x_initial(jax.random.fold_in(arg_keys[4], 71), 0),
        "sp2_choices": draw_sp2_choices(jax.random.fold_in(arg_keys[4], 71), 0),
        "domain_blocks": draw_domain_blocks(jax.random.fold_in(arg_keys[4], 71), 0),
        "basis_values": bell_draw(arg_keys[3], (DOMAINS, NPT, DBLK * BS), (DBLK * BS // 2) ** -0.5, 0.25, ((0, 128),)),
    }


HIGHEST_PRECISION = lax.Precision.HIGHEST


def pair_product(left_block, right_block, left_turned, right_turned):
    pattern = ("rba" if left_turned else "rab") + "," + ("rcb" if right_turned else "rbc") + "->rac"
    return jnp.einsum(pattern, left_block, right_block, precision=HIGHEST_PRECISION)


def square_lower(padded, row_count):
    results = []
    for diag_gap in range(3):
        summed = jnp.zeros((row_count,) + padded.shape[2:], jnp.float32)
        for middle_gap in range(-2, 3 - diag_gap):
            if middle_gap <= 0:
                left_block = padded[2:2 + row_count, 2 + middle_gap]
                left_turned = False
            else:
                left_block = padded[2 + middle_gap:2 + middle_gap + row_count, 2 - middle_gap]
                left_turned = True
            outer_gap = middle_gap + diag_gap
            if outer_gap >= 0:
                right_block = padded[2 + middle_gap:2 + middle_gap + row_count, 2 - outer_gap]
                right_turned = False
            else:
                right_block = padded[2 - diag_gap:2 - diag_gap + row_count, 2 + outer_gap]
                right_turned = True
            summed = summed + pair_product(left_block, right_block, left_turned, right_turned)
        results.append(summed)
    return jnp.stack([results[2], results[1], results[0]], axis=1)


def domain_terms(basis_row, density_tile, block_count):
    points = basis_row.shape[0]
    blocks_here = density_tile.shape[0]
    block_width = density_tile.shape[2]
    live_mask = (jnp.arange(blocks_here) < block_count).astype(basis_row.dtype)
    shaped = basis_row.reshape(points, blocks_here, block_width) * live_mask[None, :, None]
    shaped_wide = shaped.astype(jnp.float32)
    tile_wide = density_tile.astype(jnp.float32)
    density = jnp.zeros((points,), jnp.float32)
    for diag_gap in range(3):
        weight = 1.0 if diag_gap == 0 else 2.0
        applied = jnp.einsum("pkb,kbc->pkc", shaped_wide[:, diag_gap:], tile_wide[diag_gap:, 2 - diag_gap], precision=HIGHEST_PRECISION)
        density = density + weight * jnp.sum(applied * shaped_wide[:, :blocks_here - diag_gap], axis=(1, 2))
    potential = jnp.tanh(density)
    factor = blocks_here * block_width / points
    scaled = ((factor * potential)[:, None, None] * shaped_wide).astype(jnp.bfloat16)
    scaled = lax.optimization_barrier(scaled).astype(jnp.float32)
    pieces = []
    for diag_gap in range(3):
        block_sum = jnp.einsum("pkb,pkc->kbc", scaled[:, diag_gap:], shaped_wide[:, :blocks_here - diag_gap], precision=HIGHEST_PRECISION)
        filler = jnp.zeros((diag_gap, block_width, block_width), jnp.float32)
        pieces.append(jnp.concatenate([filler, block_sum], axis=0))
    return potential, jnp.stack([pieces[2], pieces[1], pieces[0]], axis=1)


def reference(x_initial, sp2_choices, domain_blocks, basis_values):
    row_total = x_initial.shape[0]
    lower_band = x_initial
    for iteration in range(ITERS):
        narrow = lax.optimization_barrier(lower_band.astype(jnp.bfloat16))
        padded = jnp.pad(narrow.astype(jnp.float32), ((2, 2), (0, 0), (0, 0), (0, 0)))
        squared = square_lower(padded, row_total)
        lower_band = jnp.where(sp2_choices[iteration] == 1, 2.0 * lower_band - squared, squared)
    rounded = lax.optimization_barrier(lower_band.astype(jnp.bfloat16))
    tile_source = jnp.pad(rounded, ((0, DBLK), (0, 0), (0, 0), (0, 0)))
    counts = jnp.sum((domain_blocks >= 0).astype(jnp.int32), axis=1).astype(jnp.int32)
    starts = domain_blocks[:, 0].astype(jnp.int32)

    def visit_domain(hamiltonian, domain_item):
        first_block, block_count, basis_row = domain_item
        density_tile = lax.dynamic_slice_in_dim(tile_source, first_block, DBLK, 0)
        potential, partial_value = domain_terms(basis_row, density_tile, block_count)
        current = lax.dynamic_slice_in_dim(hamiltonian, first_block, DBLK, 0)
        hamiltonian = lax.dynamic_update_slice_in_dim(hamiltonian, current + partial_value, first_block, 0)
        return hamiltonian, potential

    initial_sum = jnp.zeros((row_total + DBLK,) + lower_band.shape[1:], jnp.float32)
    hamiltonian, potentials = lax.scan(visit_domain, initial_sum, (starts, counts, basis_values))
    return lower_band, hamiltonian[:row_total], potentials
```

```python
import functools

import jax
import jax.numpy as jnp
from jax import lax
from jax.experimental import pallas as pl
from jax.experimental.pallas import tpu as pltpu
from jax.sharding import PartitionSpec as P


DBLK = 5
ITERS = 4
BS = 256
TILE = 256
SLOT_MOVES = (0, 1, -1, 2, -2)
OWN_PLACE, STARTS, COUNTS, MOVES, TABLE = 0, 1, 6, 11, 16

NN = (((1,), (0,)), ((), ()))
NT = (((1,), (1,)), ((), ()))
TN = (((0,), (0,)), ((), ()))


def passed_along(x, axis, by):
    count = lax.axis_size(axis)
    pairs = [(i, i + by) for i in range(count) if 0 <= i + by < count]
    return lax.ppermute(x, axis, pairs)


def dot32(a, b, dims):
    return lax.dot_general(a, b, dims, preferred_element_type=jnp.float32)


def square_kernel(choice_ref, x_ref, narrow_ref, top_ref, bottom_ref, x_out, narrow_out, ext):
    rows = narrow_ref.shape[0]
    row = pl.program_id(0)

    @pl.when(row == 0)
    def _():
        ext[0, 2] = top_ref[0]
        ext[1, 1] = top_ref[1]
        ext[1, 2] = top_ref[2]
        ext[rows + 2, 0] = bottom_ref[0]
        ext[rows + 2, 1] = bottom_ref[1]
        ext[rows + 3, 0] = bottom_ref[2]
        for r in range(rows):
            ext[r + 2] = narrow_ref[r]

    i = row + 2

    def blk(r, q):
        return ext[r, q]

    here = [blk(i, q) for q in range(3)]
    up1, up0 = blk(i - 1, 1), blk(i - 1, 2)
    upup = blk(i - 2, 2)
    dn1, dn0 = blk(i + 1, 1), blk(i + 1, 0)
    dd = blk(i + 2, 0)
    diag = (
        dot32(here[0], here[0], NT)
        + dot32(here[1], here[1], NT)
        + dot32(here[2], here[2], NT)
        + dot32(dn1, dn1, TN)
        + dot32(dd, dd, TN)
    )
    near = (
        dot32(here[0], up1, NT)
        + dot32(here[1], up0, NN)
        + dot32(here[2], here[1], NN)
        + dot32(dn1, dn0, TN)
    )
    far = dot32(here[0], upup, NN) + dot32(here[1], up1, NN) + dot32(here[2], here[0], NN)
    twice = choice_ref[0] == 1
    for q, squared in ((0, far), (1, near), (2, diag)):
        new = jnp.where(twice, 2.0 * x_ref[0, q] - squared, squared)
        x_out[0, q] = new
        narrow_out[0, q] = new.astype(jnp.bfloat16)


def square_step(choice, x, narrow, top, bottom):
    rows = x.shape[0]
    per_row = pl.BlockSpec((1, 3, BS, BS), lambda r: (r, 0, 0, 0))
    whole = pl.BlockSpec(memory_space=pltpu.VMEM)
    return pl.pallas_call(
        square_kernel,
        grid=(rows,),
        in_specs=[pl.BlockSpec(memory_space=pltpu.SMEM), per_row, whole, whole, whole],
        out_specs=[per_row, per_row],
        out_shape=[
            pltpu.HBM(x.shape, jnp.float32),
            jax.ShapeDtypeStruct(x.shape, jnp.bfloat16),
        ],
        scratch_shapes=[pltpu.VMEM((rows + 4, 3, BS, BS), jnp.bfloat16)],
        compiler_params=pltpu.CompilerParams(vmem_limit_bytes=24 << 20),
        cost_estimate=pl.CostEstimate(
            flops=rows * 12 * 2 * BS**3, bytes_accessed=x.size * 12, transcendentals=0
        ),
        name="square_step",
    )(choice, pltpu.with_memory_space_constraint(x, pltpu.HBM), narrow, top, bottom)


def plan_kernel(moves, geometry, blocks_ref, basis_ref, *refs):
    *outs, table_ref, buf, in_sems, out_sems = refs
    rows, band_count, grid_count = geometry
    local = basis_ref.shape[0]
    band = lax.axis_index("band")
    grid = lax.axis_index("grid")
    device = band * grid_count + grid
    own_moves = []
    for d in range(local):
        first = blocks_ref[0, device * local + d]
        own_moves.append(first // (rows * grid_count) - band)

    def place_of(move):
        place = jnp.int32(0)
        for d in range(local):
            place = jnp.where(own_moves[d] == move, d, place)
        return place

    for n, move in enumerate(moves):
        pltpu.make_async_copy(basis_ref.at[place_of(move)], buf.at[n], in_sems.at[n]).start()
    table_ref[OWN_PLACE] = place_of(0)
    for slot, move in enumerate(SLOT_MOVES):
        source = band - move
        live = (source >= 0) & (source < band_count)
        source = jnp.clip(source, 0, band_count - 1) * grid_count + grid
        start = jnp.int32(0)
        count = jnp.int32(0)
        for d in range(local):
            first = blocks_ref[0, source * local + d]
            match = live & (first // rows == device)
            blocks = jnp.int32(0)
            for k in range(DBLK):
                blocks += jnp.where(blocks_ref[k, source * local + d] >= 0, 1, 0)
            start = jnp.where(match, first - device * rows, start)
            count = jnp.where(match, blocks, count)
        table_ref[STARTS + slot] = start
        table_ref[COUNTS + slot] = count
    for d in range(local):
        table_ref[MOVES + d] = own_moves[d]
    for n, move in enumerate(moves):
        pltpu.make_async_copy(basis_ref.at[place_of(move)], buf.at[n], in_sems.at[n]).wait()
        pltpu.make_async_copy(buf.at[n], outs[n], out_sems.at[n]).start()
    for n, move in enumerate(moves):
        pltpu.make_async_copy(buf.at[n], outs[n], out_sems.at[n]).wait()


def plan_step(moves, blocks, basis, rows, band_count, grid_count):
    any_space = pl.BlockSpec(memory_space=pl.ANY)
    smem = pl.BlockSpec(memory_space=pltpu.SMEM)
    one = jax.ShapeDtypeStruct(basis.shape[1:], basis.dtype)
    return pl.pallas_call(
        functools.partial(plan_kernel, moves, (rows, band_count, grid_count)),
        in_specs=[smem, pl.BlockSpec(memory_space=pltpu.HBM)],
        out_specs=[any_space] * len(moves) + [smem],
        out_shape=[one] * len(moves) + [jax.ShapeDtypeStruct((TABLE,), jnp.int32)],
        scratch_shapes=[
            pltpu.VMEM((len(moves),) + basis.shape[1:], basis.dtype),
            pltpu.SemaphoreType.DMA((len(moves),)),
            pltpu.SemaphoreType.DMA((len(moves),)),
        ],
        compiler_params=pltpu.CompilerParams(vmem_limit_bytes=16 << 20),
        name="plan_step",
    )(blocks, basis)


def pick_kernel(moves, cuts, table_ref, basis_ref, *refs):
    *outs, buf, in_sems, out_sems = refs
    local = basis_ref.shape[0]

    def place_of(move):
        place = jnp.int32(0)
        for d in range(local):
            place = jnp.where(table_ref[MOVES + d] == move, d, place)
        return place

    def load(n):
        return pltpu.make_async_copy(basis_ref.at[place_of(moves[n])], buf.at[n], in_sems.at[n])

    def stores(n):
        return [
            pltpu.make_async_copy(
                buf.at[n, pl.ds(low, high - low)],
                outs[n * len(cuts) + c],
                out_sems.at[n * len(cuts) + c],
            )
            for c, (low, high) in enumerate(cuts)
        ]

    for n in range(len(moves)):
        load(n).start()
    for n in range(len(moves)):
        load(n).wait()
        for copy in stores(n):
            copy.start()
    for n in range(len(moves)):
        for copy in stores(n):
            copy.wait()


def pick_step(moves, cuts, table, basis):
    any_space = pl.BlockSpec(memory_space=pl.ANY)
    smem = pl.BlockSpec(memory_space=pltpu.SMEM)
    width = basis.shape[2]
    outs = [jax.ShapeDtypeStruct((high - low, width), basis.dtype) for low, high in cuts]
    return pl.pallas_call(
        functools.partial(pick_kernel, moves, cuts),
        in_specs=[smem, pl.BlockSpec(memory_space=pltpu.HBM)],
        out_specs=[any_space] * (len(moves) * len(cuts)),
        out_shape=outs * len(moves),
        scratch_shapes=[
            pltpu.VMEM((len(moves),) + basis.shape[1:], basis.dtype),
            pltpu.SemaphoreType.DMA((len(moves),)),
            pltpu.SemaphoreType.DMA((len(moves) * len(cuts),)),
        ],
        compiler_params=pltpu.CompilerParams(vmem_limit_bytes=16 << 20),
        name="pick_step",
    )(table, basis)


def fill_stack(tile_ref, stack):
    rows = tile_ref.shape[0]
    for r in range(rows):
        stack[r, 0:BS] = tile_ref[r, 2]
        for gap in (1, 2):
            where = pl.ds(gap * BS, BS)
            if r + gap < rows:
                stack[r, where] = tile_ref[r + gap, 2 - gap] * 2
            else:
                stack[r, where] = jnp.zeros((BS, BS), jnp.bfloat16)


def blank_tail(phi, slot, blocks):
    for k in range(2, DBLK):

        @pl.when(k >= blocks)
        def _():
            phi[slot, :, k * BS : (k + 1) * BS] = jnp.zeros((phi.shape[1], BS), jnp.bfloat16)


def potential_of_slot(phi, slot, first, stack, pot_out, psi_at, factor):
    points = phi.shape[1]
    rows = stack.shape[0]

    @pl.loop(0, points // TILE)
    def _(step):
        here = pl.ds(pl.multiple_of(step * TILE, TILE), TILE)
        total = jnp.zeros((TILE, BS), jnp.float32)
        for j in range(DBLK):
            last = min(j + 3, DBLK)
            row = jnp.minimum(first + j, rows - 1)
            applied = dot32(phi[slot, here, j * BS : last * BS], stack[row, 0 : (last - j) * BS], NN)
            total += applied * phi[slot, here, j * BS : (j + 1) * BS].astype(jnp.float32)
        potential = jnp.tanh(jnp.sum(total, axis=1, keepdims=True))
        spread = jnp.transpose(jnp.broadcast_to(potential, (TILE, 128)))
        pot_out[slot, :, here] = spread[0:1]
        scale = factor * potential
        psi_at(here)[...] = (scale * phi[slot, here, :].astype(jnp.float32)).astype(jnp.bfloat16)


def add_blocks(ham, psi, phi, slot, first, blocks):
    for k in range(DBLK):

        @pl.when(k < blocks)
        def _():
            low = max(0, k - 2)
            piece = dot32(psi[:, k * BS : (k + 1) * BS], phi[slot, :, low * BS : (k + 1) * BS], TN)
            for j in range(low, k + 1):
                ham[first + k, 2 - (k - j)] += piece[:, (j - low) * BS : (j - low + 1) * BS]


def domain_kernel(slots, has_base, factor, table_ref, tile_ref, *refs):
    refs = list(refs)
    base_ref = refs.pop(0) if has_base else None
    basis_refs = [refs.pop(0) for _ in slots]
    ham_out, pot_out, phi, psi, stack, ham, sems, base_sem = refs

    def fetch(n):
        source = basis_refs[n]
        if len(source.shape) == 3:
            source = source.at[table_ref[OWN_PLACE]]
        return pltpu.make_async_copy(source, phi.at[n], sems.at[n])

    for n in range(len(slots)):
        fetch(n).start()
    if has_base:
        base = pltpu.make_async_copy(base_ref, ham, base_sem)
        base.start()
    else:
        ham[...] = jnp.zeros_like(ham)
    fill_stack(tile_ref, stack)
    pot_out[...] = jnp.zeros_like(pot_out)
    for n in range(len(slots)):
        fetch(n).wait()
    if has_base:
        base.wait()

    @pl.loop(0, len(slots))
    def _(n):
        first = table_ref[STARTS + slots[0] + n]
        blocks = table_ref[COUNTS + slots[0] + n]

        @pl.when(blocks > 0)
        def _():
            blank_tail(phi, n, blocks)
            potential_of_slot(phi, n, first, stack, pot_out, lambda here: psi.at[here], factor)
            add_blocks(ham, psi, phi, n, first, blocks)

    result = pltpu.make_async_copy(ham, ham_out, base_sem)
    result.start()
    result.wait()


def domain_step(slots, table, tiles, base, arrays, factor):
    rows = tiles.shape[0]
    points, width = arrays[-1].shape[-2:]
    number = len(arrays)
    has_base = base is not None
    smem = pl.BlockSpec(memory_space=pltpu.SMEM)
    vmem = pl.BlockSpec(memory_space=pltpu.VMEM)
    hbm = pl.BlockSpec(memory_space=pl.ANY)
    operands = [table, tiles] + ([base] if has_base else []) + list(arrays)
    return pl.pallas_call(
        functools.partial(domain_kernel, slots, has_base, factor),
        in_specs=[smem, vmem]
        + [pl.BlockSpec(memory_space=pltpu.HBM) if o.ndim >= 3 else hbm for o in operands[2:]],
        out_specs=[pl.BlockSpec(memory_space=pltpu.HBM), vmem],
        out_shape=[
            pltpu.HBM((rows, 3, BS, BS), jnp.float32),
            jax.ShapeDtypeStruct((number, 1, points), jnp.float32),
        ],
        scratch_shapes=[
            pltpu.VMEM((number, points, width), jnp.bfloat16),
            pltpu.VMEM((points, width), jnp.bfloat16),
            pltpu.VMEM((rows, 3 * BS, BS), jnp.bfloat16),
            pltpu.VMEM((rows, 3, BS, BS), jnp.float32),
            pltpu.SemaphoreType.DMA((number,)),
            pltpu.SemaphoreType.DMA,
        ],
        compiler_params=pltpu.CompilerParams(vmem_limit_bytes=36 << 20),
        cost_estimate=pl.CostEstimate(
            flops=number * 24 * 2 * points * BS * BS,
            bytes_accessed=number * points * width * 2 + rows * 3 * BS * BS * 6,
            transcendentals=number * points,
        ),
        name="domain_step",
    )(*operands)


def potential_kernel(slots, factor, table_ref, tile_ref, *refs):
    basis_refs = refs[: len(slots)]
    psi_out, pot_out, phi, stack = refs[len(slots) :]
    fill_stack(tile_ref, stack)
    pot_out[...] = jnp.zeros_like(pot_out)
    for n in range(len(slots)):
        phi[n] = basis_refs[n][...]

    @pl.loop(0, len(slots))
    def _(n):
        first = table_ref[STARTS + slots[0] + n]
        blocks = table_ref[COUNTS + slots[0] + n]

        @pl.when(blocks > 0)
        def _():
            blank_tail(phi, n, blocks)
            potential_of_slot(phi, n, first, stack, pot_out, lambda here: psi_out.at[n, here], factor)


def potential_step(slots, table, tiles, arrays, factor):
    rows = tiles.shape[0]
    points, width = arrays[-1].shape
    number = len(arrays)
    smem = pl.BlockSpec(memory_space=pltpu.SMEM)
    vmem = pl.BlockSpec(memory_space=pltpu.VMEM)
    hbm = pl.BlockSpec(memory_space=pl.ANY)
    return pl.pallas_call(
        functools.partial(potential_kernel, slots, factor),
        in_specs=[smem, vmem] + [vmem] * number,
        out_specs=[vmem, vmem],
        out_shape=[
            jax.ShapeDtypeStruct((number, points, width), jnp.bfloat16),
            jax.ShapeDtypeStruct((number, 1, points), jnp.float32),
        ],
        scratch_shapes=[
            pltpu.VMEM((number, points, width), jnp.bfloat16),
            pltpu.VMEM((rows, 3 * BS, BS), jnp.bfloat16),
        ],
        compiler_params=pltpu.CompilerParams(vmem_limit_bytes=16 << 20),
        cost_estimate=pl.CostEstimate(
            flops=number * 12 * 2 * points * BS * BS,
            bytes_accessed=number * points * width * 4,
            transcendentals=number * points,
        ),
        name="potential_step",
    )(table, tiles, *arrays)


def block_kernel(slots, table_ref, psi_ref, base_ref, *refs):
    basis_refs = refs[: len(slots)]
    ham_out, ham, sems = refs[len(slots) :]
    rows = ham.shape[0]

    def send(r):
        return pltpu.make_async_copy(ham.at[r], ham_out.at[r], sems.at[r])

    for r in range(rows):
        ham[r] = base_ref[r]
        for n, slot in enumerate(slots):
            k = r - table_ref[STARTS + slot]
            blocks = table_ref[COUNTS + slot]

            @pl.when((k >= 0) & (k < blocks))
            def _():
                left = psi_ref[n, :, pl.ds(pl.multiple_of(k * BS, BS), BS)]
                for gap in range(3):

                    @pl.when(k >= gap)
                    def _():
                        where = pl.ds(pl.multiple_of((k - gap) * BS, BS), BS)
                        ham[r, 2 - gap] += dot32(left, basis_refs[n][:, where], TN)

        send(r).start()
    for r in range(rows):
        send(r).wait()


def block_step(slots, table, psi, base, arrays):
    number, points, width = psi.shape
    rows = base.shape[0]
    smem = pl.BlockSpec(memory_space=pltpu.SMEM)
    vmem = pl.BlockSpec(memory_space=pltpu.VMEM)
    return pl.pallas_call(
        functools.partial(block_kernel, slots),
        in_specs=[smem, vmem, vmem] + [vmem] * number,
        out_specs=pl.BlockSpec(memory_space=pltpu.HBM),
        out_shape=pltpu.HBM(base.shape, jnp.float32),
        scratch_shapes=[
            pltpu.VMEM(base.shape, jnp.float32),
            pltpu.SemaphoreType.DMA((rows,)),
        ],
        compiler_params=pltpu.CompilerParams(vmem_limit_bytes=20 << 20),
        cost_estimate=pl.CostEstimate(
            flops=number * 12 * 2 * points * BS * BS,
            bytes_accessed=number * points * width * 4 + base.size * 8,
            transcendentals=0,
        ),
        name="block_step",
    )(table, psi, base, *arrays)


def whole_step(x_initial, sp2_choices, domain_blocks, basis_values):
    row_count = x_initial.shape[0]
    band_count = lax.axis_size("band")
    grid_count = lax.axis_size("grid")
    local_domains, points, width = basis_values.shape
    factor = width / points
    cuts = ((0, 512), (512, points))

    def orbitals(value, move):
        return passed_along(value, "band", move)

    basis_values = pltpu.with_memory_space_constraint(basis_values, pltpu.HBM)
    blocks = pltpu.with_memory_space_constraint(domain_blocks.T, pltpu.HBM)
    plus, minus, table = plan_step(
        (1, -1), blocks, basis_values, row_count, band_count, grid_count
    )
    near = [orbitals(plus, 1), orbitals(minus, -1)]
    plus_a, plus_b, minus_a, minus_b = pick_step((2, -2), cuts, table, basis_values)
    far_a = [orbitals(plus_a, 2), orbitals(minus_a, -2)]
    far_b = [orbitals(plus_b, 2), orbitals(minus_b, -2)]

    x = x_initial
    narrow = x.astype(jnp.bfloat16)
    for iteration in range(ITERS):
        upward = jnp.stack([narrow[-2, 2], narrow[-1, 1], narrow[-1, 2]])
        downward = jnp.stack([narrow[0, 0], narrow[0, 1], narrow[1, 0]])
        top = passed_along(upward, ("band", "grid"), 1)
        bottom = passed_along(downward, ("band", "grid"), -1)
        x, narrow = square_step(sp2_choices[iteration : iteration + 1], x, narrow, top, bottom)

    ham, near_pot = domain_step((0, 1, 2), table, narrow, None, [basis_values] + near, factor)
    ham, pot_a = domain_step((3, 4), table, narrow, ham, far_a, factor)
    psi_b, pot_b = potential_step((3, 4), table, narrow, far_b, factor)
    far_pot = jnp.concatenate([pot_a[:, 0], pot_b[:, 0]], axis=1)
    ham = block_step((3, 4), table, psi_b, ham, far_b)
    sent_back = [near_pot[0, 0]]
    for move, values in ((1, near_pot[1, 0]), (-1, near_pot[2, 0]), (2, far_pot[0]), (-2, far_pot[1])):
        sent_back.append(passed_along(values, "band", -move))
    own_moves = table[MOVES : MOVES + local_domains]
    own_potential = jnp.zeros((local_domains, points), jnp.float32)
    for move, values in zip(SLOT_MOVES, sent_back):
        own_potential = jnp.where((own_moves == move)[:, None], values[None, :], own_potential)
    return x, ham, own_potential


def solution(mesh):
    placed = (P(("band", "grid"), None, None, None), P(), P(), P(("band", "grid"), None, None))
    return jax.shard_map(
        whole_step,
        mesh=mesh,
        in_specs=placed,
        out_specs=(
            P(("band", "grid"), None, None, None),
            P(("band", "grid"), None, None, None),
            P(("band", "grid"), None),
        ),
        check_vma=False,
    )
```

```python
import functools

import jax
import jax.numpy as jnp
from jax import lax
from jax.experimental import pallas as pl
from jax.experimental.pallas import tpu as pltpu
from jax.sharding import PartitionSpec as P


DBLK = 5
ITERS = 4
BS = 256
TILE = 256
SLOT_MOVES = (0, 1, -1, 2, -2)
OWN_PLACE, STARTS, COUNTS, MOVES, TABLE = 0, 1, 6, 11, 16

NN = (((1,), (0,)), ((), ()))
NT = (((1,), (1,)), ((), ()))
TN = (((0,), (0,)), ((), ()))


def passed_along(x, axis, by):
    count = lax.axis_size(axis)
    pairs = [(i, i + by) for i in range(count) if 0 <= i + by < count]
    return lax.ppermute(x, axis, pairs)


def dot32(a, b, dims):
    return lax.dot_general(a, b, dims, preferred_element_type=jnp.float32)


def edge_blocks(rows):
    return ((0, 0), (0, 1), (1, 0), (rows - 2, 2), (rows - 1, 1), (rows - 1, 2))


def local_kernel(
    choice_ref, x_ref, edge_ref, narrow_ref, down_ref, up_ref, x_out, narrow_out, ext
):
    rows = narrow_ref.shape[0]
    edges = edge_blocks(rows)
    none = jnp.zeros((BS, BS), jnp.bfloat16)
    for r in (0, 1, rows + 2, rows + 3):
        for q in range(3):
            ext[r, q] = none
    for r in range(rows):
        for q in range(3):
            if (r, q) in edges:
                place = edges.index((r, q))
                ext[r + 2, q] = down_ref[place] if place < 3 else up_ref[place - 3]
            else:
                ext[r + 2, q] = narrow_ref[r, q]
    twice = choice_ref[0] == 1

    @pl.loop(0, rows)
    def _(row):
        i = row + 2
        here = [ext[i, q] for q in range(3)]
        up1, up0 = ext[i - 1, 1], ext[i - 1, 2]
        upup = ext[i - 2, 2]
        dn1, dn0 = ext[i + 1, 1], ext[i + 1, 0]
        dd = ext[i + 2, 0]
        diag = (
            dot32(here[0], here[0], NT)
            + dot32(here[1], here[1], NT)
            + dot32(here[2], here[2], NT)
            + dot32(dn1, dn1, TN)
            + dot32(dd, dd, TN)
        )
        near = (
            dot32(here[0], up1, NT)
            + dot32(here[1], up0, NN)
            + dot32(here[2], here[1], NN)
            + dot32(dn1, dn0, TN)
        )
        far = dot32(here[0], upup, NN) + dot32(here[1], up1, NN) + dot32(here[2], here[0], NN)
        for q, squared in ((0, far), (1, near), (2, diag)):
            new = jnp.where(twice, 2.0 * x_ref[row, q] - squared, squared)
            x_out[row, q] = new
            narrow_out[row, q] = new.astype(jnp.bfloat16)

    @pl.when(twice)
    def _():
        for place, (r, q) in enumerate(edges):
            x_out[r, q] += 2.0 * (edge_ref[place] - x_ref[r, q])


def local_step(choice, x, edge, narrow, down, up):
    rows = x.shape[0]
    vmem = pl.BlockSpec(memory_space=pltpu.VMEM)
    return pl.pallas_call(
        local_kernel,
        in_specs=[pl.BlockSpec(memory_space=pltpu.SMEM)] + [vmem] * 5,
        out_specs=[vmem, vmem],
        out_shape=[
            jax.ShapeDtypeStruct(x.shape, jnp.float32),
            jax.ShapeDtypeStruct(x.shape, jnp.bfloat16),
        ],
        scratch_shapes=[pltpu.VMEM((rows + 4, 3, BS, BS), jnp.bfloat16)],
        compiler_params=pltpu.CompilerParams(vmem_limit_bytes=22 << 20),
        cost_estimate=pl.CostEstimate(
            flops=rows * 12 * 2 * BS**3, bytes_accessed=x.size * 4, transcendentals=0
        ),
        name="local_step",
    )(choice, x, edge, narrow, down, up)


def border_kernel(
    choice_ref, before_ref, top_ref, bottom_ref, x_ref, edge_out, down_out, up_out
):
    rows = x_ref.shape[0]
    sign = jnp.where(choice_ref[0] == 1, -1.0, 1.0)
    x00, x01, x10 = before_ref[0], before_ref[1], before_ref[2]
    t_far, t_mid, t_near = top_ref[0], top_ref[1], top_ref[2]
    b_far, b_near, b_last = bottom_ref[0], bottom_ref[1], bottom_ref[2]
    added = (
        lambda: dot32(x00, t_far, NN) + dot32(x01, t_mid, NN),
        lambda: dot32(x00, t_mid, NT) + dot32(x01, t_near, NN),
        lambda: dot32(x10, t_near, NN),
        lambda: dot32(b_far, b_far, TN),
        lambda: dot32(b_near, b_far, TN),
        lambda: dot32(b_near, b_near, TN) + dot32(b_last, b_last, TN),
    )
    for place, (r, q) in enumerate(edge_blocks(rows)):
        new = x_ref[r, q] + sign * added[place]()
        edge_out[place] = new
        if place < 3:
            down_out[place] = new.astype(jnp.bfloat16)
        else:
            up_out[place - 3] = new.astype(jnp.bfloat16)


def border_step(choice, before, top, bottom, x):
    vmem = pl.BlockSpec(memory_space=pltpu.VMEM)
    edge = jax.ShapeDtypeStruct(top.shape, jnp.bfloat16)
    return pl.pallas_call(
        border_kernel,
        in_specs=[pl.BlockSpec(memory_space=pltpu.SMEM)] + [vmem] * 4,
        out_specs=[vmem] * 3,
        out_shape=[jax.ShapeDtypeStruct((6, BS, BS), jnp.float32), edge, edge],
        compiler_params=pltpu.CompilerParams(vmem_limit_bytes=12 << 20),
        cost_estimate=pl.CostEstimate(
            flops=9 * 2 * BS**3, bytes_accessed=x.size, transcendentals=0
        ),
        name="border_step",
    )(choice, before, top, bottom, x)


def density_kernel(x_ref, edge_ref, out, sems):
    rows = x_ref.shape[0]
    edges = edge_blocks(rows)
    copies = []
    for r in range(rows):
        for q in range(3):
            source = edge_ref.at[edges.index((r, q))] if (r, q) in edges else x_ref.at[r, q]
            copies.append(pltpu.make_async_copy(source, out.at[r, q], sems.at[r * 3 + q]))
    for copy in copies:
        copy.start()
    for copy in copies:
        copy.wait()


def density_step(x, edge):
    vmem = pl.BlockSpec(memory_space=pltpu.VMEM)
    return pl.pallas_call(
        density_kernel,
        in_specs=[vmem, vmem],
        out_specs=pl.BlockSpec(memory_space=pltpu.HBM),
        out_shape=pltpu.HBM(x.shape, jnp.float32),
        scratch_shapes=[pltpu.SemaphoreType.DMA((x.shape[0] * 3,))],
        compiler_params=pltpu.CompilerParams(vmem_limit_bytes=8 << 20),
        cost_estimate=pl.CostEstimate(flops=0, bytes_accessed=x.size * 4, transcendentals=0),
        name="density_step",
    )(x, edge)


def plan_kernel(moves, geometry, blocks_ref, basis_ref, *refs):
    *outs, table_ref, buf, in_sems, out_sems = refs
    rows, band_count, grid_count = geometry
    local = basis_ref.shape[0]
    band = lax.axis_index("band")
    grid = lax.axis_index("grid")
    device = band * grid_count + grid
    own_moves = []
    for d in range(local):
        first = blocks_ref[0, device * local + d]
        own_moves.append(first // (rows * grid_count) - band)

    def place_of(move):
        place = jnp.int32(0)
        for d in range(local):
            place = jnp.where(own_moves[d] == move, d, place)
        return place

    for n, move in enumerate(moves):
        pltpu.make_async_copy(basis_ref.at[place_of(move)], buf.at[n], in_sems.at[n]).start()
    table_ref[OWN_PLACE] = place_of(0)
    for slot, move in enumerate(SLOT_MOVES):
        source = band - move
        live = (source >= 0) & (source < band_count)
        source = jnp.clip(source, 0, band_count - 1) * grid_count + grid
        start = jnp.int32(0)
        count = jnp.int32(0)
        for d in range(local):
            first = blocks_ref[0, source * local + d]
            match = live & (first // rows == device)
            blocks = jnp.int32(0)
            for k in range(DBLK):
                blocks += jnp.where(blocks_ref[k, source * local + d] >= 0, 1, 0)
            start = jnp.where(match, first - device * rows, start)
            count = jnp.where(match, blocks, count)
        table_ref[STARTS + slot] = start
        table_ref[COUNTS + slot] = count
    for d in range(local):
        table_ref[MOVES + d] = own_moves[d]
    for n, move in enumerate(moves):
        pltpu.make_async_copy(basis_ref.at[place_of(move)], buf.at[n], in_sems.at[n]).wait()
        pltpu.make_async_copy(buf.at[n], outs[n], out_sems.at[n]).start()
    for n, move in enumerate(moves):
        pltpu.make_async_copy(buf.at[n], outs[n], out_sems.at[n]).wait()


def plan_step(moves, blocks, basis, rows, band_count, grid_count):
    any_space = pl.BlockSpec(memory_space=pl.ANY)
    smem = pl.BlockSpec(memory_space=pltpu.SMEM)
    one = jax.ShapeDtypeStruct(basis.shape[1:], basis.dtype)
    return pl.pallas_call(
        functools.partial(plan_kernel, moves, (rows, band_count, grid_count)),
        in_specs=[smem, pl.BlockSpec(memory_space=pltpu.HBM)],
        out_specs=[any_space] * len(moves) + [smem],
        out_shape=[one] * len(moves) + [jax.ShapeDtypeStruct((TABLE,), jnp.int32)],
        scratch_shapes=[
            pltpu.VMEM((len(moves),) + basis.shape[1:], basis.dtype),
            pltpu.SemaphoreType.DMA((len(moves),)),
            pltpu.SemaphoreType.DMA((len(moves),)),
        ],
        compiler_params=pltpu.CompilerParams(vmem_limit_bytes=16 << 20),
        name="plan_step",
    )(blocks, basis)


def pick_kernel(moves, cuts, table_ref, basis_ref, *refs):
    *outs, buf, in_sems, out_sems = refs
    local = basis_ref.shape[0]

    def place_of(move):
        place = jnp.int32(0)
        for d in range(local):
            place = jnp.where(table_ref[MOVES + d] == move, d, place)
        return place

    def load(n):
        return pltpu.make_async_copy(basis_ref.at[place_of(moves[n])], buf.at[n], in_sems.at[n])

    def stores(n):
        return [
            pltpu.make_async_copy(
                buf.at[n, pl.ds(low, high - low)],
                outs[n * len(cuts) + c],
                out_sems.at[n * len(cuts) + c],
            )
            for c, (low, high) in enumerate(cuts)
        ]

    for n in range(len(moves)):
        load(n).start()
    for n in range(len(moves)):
        load(n).wait()
        for copy in stores(n):
            copy.start()
    for n in range(len(moves)):
        for copy in stores(n):
            copy.wait()


def pick_step(moves, cuts, table, basis):
    any_space = pl.BlockSpec(memory_space=pl.ANY)
    smem = pl.BlockSpec(memory_space=pltpu.SMEM)
    width = basis.shape[2]
    outs = [jax.ShapeDtypeStruct((high - low, width), basis.dtype) for low, high in cuts]
    return pl.pallas_call(
        functools.partial(pick_kernel, moves, cuts),
        in_specs=[smem, pl.BlockSpec(memory_space=pltpu.HBM)],
        out_specs=[any_space] * (len(moves) * len(cuts)),
        out_shape=outs * len(moves),
        scratch_shapes=[
            pltpu.VMEM((len(moves),) + basis.shape[1:], basis.dtype),
            pltpu.SemaphoreType.DMA((len(moves),)),
            pltpu.SemaphoreType.DMA((len(moves) * len(cuts),)),
        ],
        compiler_params=pltpu.CompilerParams(vmem_limit_bytes=16 << 20),
        name="pick_step",
    )(table, basis)


def fill_stack(tile_refs, stack):
    main, down, up = tile_refs
    rows = main.shape[0]
    edges = edge_blocks(rows)

    def tile(r, q):
        if (r, q) not in edges:
            return main[r, q]
        place = edges.index((r, q))
        return down[place] if place < 3 else up[place - 3]

    for r in range(rows):
        stack[r, 0:BS] = tile(r, 2)
        for gap in (1, 2):
            where = pl.ds(gap * BS, BS)
            if r + gap < rows:
                stack[r, where] = tile(r + gap, 2 - gap) * 2
            else:
                stack[r, where] = jnp.zeros((BS, BS), jnp.bfloat16)


def blank_tail(phi, slot, blocks):
    for k in range(2, DBLK):

        @pl.when(k >= blocks)
        def _():
            phi[slot, :, k * BS : (k + 1) * BS] = jnp.zeros((phi.shape[1], BS), jnp.bfloat16)


def potential_of_slot(phi, slot, first, stack, pot_out, psi_at, factor):
    points = phi.shape[1]
    rows = stack.shape[0]

    @pl.loop(0, points // TILE)
    def _(step):
        here = pl.ds(pl.multiple_of(step * TILE, TILE), TILE)
        total = jnp.zeros((TILE, BS), jnp.float32)
        for j in range(DBLK):
            last = min(j + 3, DBLK)
            row = jnp.minimum(first + j, rows - 1)
            applied = dot32(phi[slot, here, j * BS : last * BS], stack[row, 0 : (last - j) * BS], NN)
            total += applied * phi[slot, here, j * BS : (j + 1) * BS].astype(jnp.float32)
        potential = jnp.tanh(jnp.sum(total, axis=1, keepdims=True))
        spread = jnp.transpose(jnp.broadcast_to(potential, (TILE, 128)))
        pot_out[slot, :, here] = spread[0:1]
        scale = factor * potential
        psi_at(here)[...] = (scale * phi[slot, here, :].astype(jnp.float32)).astype(jnp.bfloat16)


def add_blocks(ham, psi, phi, slot, first, blocks):
    for k in range(DBLK):

        @pl.when(k < blocks)
        def _():
            low = max(0, k - 2)
            piece = dot32(psi[:, k * BS : (k + 1) * BS], phi[slot, :, low * BS : (k + 1) * BS], TN)
            for j in range(low, k + 1):
                ham[first + k, 2 - (k - j)] += piece[:, (j - low) * BS : (j - low + 1) * BS]


def domain_kernel(slots, has_base, factor, table_ref, main_ref, down_ref, up_ref, *refs):
    refs = list(refs)
    base_ref = refs.pop(0) if has_base else None
    basis_refs = [refs.pop(0) for _ in slots]
    ham, pot_out, phi, psi, stack, sems = refs

    def fetch(n):
        source = basis_refs[n]
        if len(source.shape) == 3:
            source = source.at[table_ref[OWN_PLACE]]
        return pltpu.make_async_copy(source, phi.at[n], sems.at[n])

    for n in range(len(slots)):
        fetch(n).start()
    for r in range(ham.shape[0]):
        ham[r] = base_ref[r] if has_base else jnp.zeros_like(ham[r])
    fill_stack((main_ref, down_ref, up_ref), stack)
    pot_out[...] = jnp.zeros_like(pot_out)
    for n in range(len(slots)):
        fetch(n).wait()

    @pl.loop(0, len(slots))
    def _(n):
        first = table_ref[STARTS + slots[0] + n]
        blocks = table_ref[COUNTS + slots[0] + n]

        @pl.when(blocks > 0)
        def _():
            blank_tail(phi, n, blocks)
            potential_of_slot(phi, n, first, stack, pot_out, lambda here: psi.at[here], factor)
            add_blocks(ham, psi, phi, n, first, blocks)


def domain_step(slots, table, tiles, base, arrays, factor):
    rows = tiles[0].shape[0]
    points, width = arrays[-1].shape[-2:]
    number = len(arrays)
    has_base = base is not None
    smem = pl.BlockSpec(memory_space=pltpu.SMEM)
    vmem = pl.BlockSpec(memory_space=pltpu.VMEM)
    hbm = pl.BlockSpec(memory_space=pl.ANY)
    operands = [table, *tiles] + ([base] if has_base else []) + list(arrays)
    return pl.pallas_call(
        functools.partial(domain_kernel, slots, has_base, factor),
        in_specs=[smem] + [vmem] * (3 + has_base) + [hbm] * number,
        out_specs=[vmem, vmem],
        out_shape=[
            jax.ShapeDtypeStruct((rows, 3, BS, BS), jnp.float32),
            jax.ShapeDtypeStruct((number, 1, points), jnp.float32),
        ],
        scratch_shapes=[
            pltpu.VMEM((number, points, width), jnp.bfloat16),
            pltpu.VMEM((points, width), jnp.bfloat16),
            pltpu.VMEM((rows, 3 * BS, BS), jnp.bfloat16),
            pltpu.SemaphoreType.DMA((number,)),
        ],
        compiler_params=pltpu.CompilerParams(vmem_limit_bytes=(17 << 20) + number * points * width * 2),
        cost_estimate=pl.CostEstimate(
            flops=number * 24 * 2 * points * BS * BS,
            bytes_accessed=number * points * width * 2 + rows * 3 * BS * BS * 6,
            transcendentals=number * points,
        ),
        name="domain_step",
    )(*operands)


def potential_kernel(slots, factor, table_ref, main_ref, down_ref, up_ref, *refs):
    basis_refs = refs[: len(slots)]
    psi_out, pot_out, phi, stack = refs[len(slots) :]
    fill_stack((main_ref, down_ref, up_ref), stack)
    pot_out[...] = jnp.zeros_like(pot_out)
    for n in range(len(slots)):
        phi[n] = basis_refs[n][...]

    @pl.loop(0, len(slots))
    def _(n):
        first = table_ref[STARTS + slots[0] + n]
        blocks = table_ref[COUNTS + slots[0] + n]

        @pl.when(blocks > 0)
        def _():
            blank_tail(phi, n, blocks)
            potential_of_slot(phi, n, first, stack, pot_out, lambda here: psi_out.at[n, here], factor)


def potential_step(slots, table, tiles, arrays, factor):
    rows = tiles[0].shape[0]
    points, width = arrays[-1].shape
    number = len(arrays)
    smem = pl.BlockSpec(memory_space=pltpu.SMEM)
    vmem = pl.BlockSpec(memory_space=pltpu.VMEM)
    hbm = pl.BlockSpec(memory_space=pl.ANY)
    return pl.pallas_call(
        functools.partial(potential_kernel, slots, factor),
        in_specs=[smem] + [vmem] * (3 + number),
        out_specs=[vmem, vmem],
        out_shape=[
            jax.ShapeDtypeStruct((number, points, width), jnp.bfloat16),
            jax.ShapeDtypeStruct((number, 1, points), jnp.float32),
        ],
        scratch_shapes=[
            pltpu.VMEM((number, points, width), jnp.bfloat16),
            pltpu.VMEM((rows, 3 * BS, BS), jnp.bfloat16),
        ],
        compiler_params=pltpu.CompilerParams(vmem_limit_bytes=16 << 20),
        cost_estimate=pl.CostEstimate(
            flops=number * 12 * 2 * points * BS * BS,
            bytes_accessed=number * points * width * 4,
            transcendentals=number * points,
        ),
        name="potential_step",
    )(table, *tiles, *arrays)


def block_kernel(slots, table_ref, psi_ref, base_ref, *refs):
    basis_refs = refs[: len(slots)]
    ham_out, ham, sems = refs[len(slots) :]
    rows = ham.shape[0]

    def send(r):
        return pltpu.make_async_copy(ham.at[r], ham_out.at[r], sems.at[r])

    for r in range(rows):
        ham[r] = base_ref[r]
        for n, slot in enumerate(slots):
            k = r - table_ref[STARTS + slot]
            blocks = table_ref[COUNTS + slot]

            @pl.when((k >= 0) & (k < blocks))
            def _():
                left = psi_ref[n, :, pl.ds(pl.multiple_of(k * BS, BS), BS)]
                for gap in range(3):

                    @pl.when(k >= gap)
                    def _():
                        where = pl.ds(pl.multiple_of((k - gap) * BS, BS), BS)
                        ham[r, 2 - gap] += dot32(left, basis_refs[n][:, where], TN)

        send(r).start()
    for r in range(rows):
        send(r).wait()


def block_step(slots, table, psi, base, arrays):
    number, points, width = psi.shape
    rows = base.shape[0]
    smem = pl.BlockSpec(memory_space=pltpu.SMEM)
    vmem = pl.BlockSpec(memory_space=pltpu.VMEM)
    return pl.pallas_call(
        functools.partial(block_kernel, slots),
        in_specs=[smem, vmem, vmem] + [vmem] * number,
        out_specs=pl.BlockSpec(memory_space=pltpu.HBM),
        out_shape=pltpu.HBM(base.shape, jnp.float32),
        scratch_shapes=[
            pltpu.VMEM(base.shape, jnp.float32),
            pltpu.SemaphoreType.DMA((rows,)),
        ],
        compiler_params=pltpu.CompilerParams(vmem_limit_bytes=20 << 20),
        cost_estimate=pl.CostEstimate(
            flops=number * 12 * 2 * points * BS * BS,
            bytes_accessed=number * points * width * 4 + base.size * 8,
            transcendentals=0,
        ),
        name="block_step",
    )(table, psi, base, *arrays)


def whole_step(x_initial, sp2_choices, domain_blocks, basis_values):
    row_count = x_initial.shape[0]
    band_count = lax.axis_size("band")
    grid_count = lax.axis_size("grid")
    local_domains, points, width = basis_values.shape
    factor = width / points
    cuts = ((0, 512), (512, points))

    def orbitals(value, move):
        return passed_along(value, "band", move)

    basis_values = pltpu.with_memory_space_constraint(basis_values, pltpu.HBM)
    blocks = pltpu.with_memory_space_constraint(domain_blocks.T, pltpu.HBM)
    plus, minus, table = plan_step(
        (2, -2), blocks, basis_values, row_count, band_count, grid_count
    )
    halfway = [orbitals(plus, 1), orbitals(minus, -1)]
    plus, minus = pick_step((1, -1), ((0, points),), table, basis_values)
    near = [orbitals(plus, 1), orbitals(minus, -1)]
    far_a = [orbitals(halfway[n][: cuts[0][1]], 1 - 2 * n) for n in (0, 1)]
    far_b = [orbitals(halfway[n][cuts[1][0] :], 1 - 2 * n) for n in (0, 1)]

    x = x_initial
    narrow = x.astype(jnp.bfloat16)
    upward = jnp.stack([narrow[-2, 2], narrow[-1, 1], narrow[-1, 2]])
    downward = jnp.stack([narrow[0, 0], narrow[0, 1], narrow[1, 0]])
    edge = jnp.stack([x[r, q] for r, q in edge_blocks(row_count)])
    for iteration in range(ITERS):
        choice = sp2_choices[iteration : iteration + 1]
        top = passed_along(upward, ("band", "grid"), 1)
        bottom = passed_along(downward, ("band", "grid"), -1)
        before = downward
        x, narrow = local_step(choice, x, edge, narrow, downward, upward)
        edge, downward, upward = border_step(choice, before, top, bottom, x)
    tiles = (narrow, downward, upward)
    density = density_step(x, edge)

    ham, near_pot = domain_step((0, 1, 2), table, tiles, None, [basis_values] + near, factor)
    ham, pot_a = domain_step((3, 4), table, tiles, ham, far_a, factor)
    psi_b, pot_b = potential_step((3, 4), table, tiles, far_b, factor)
    far_pot = jnp.concatenate([pot_a[:, 0], pot_b[:, 0]], axis=1)
    ham = block_step((3, 4), table, psi_b, ham, far_b)
    sent_back = [near_pot[0, 0]]
    for move, values in ((1, near_pot[1, 0]), (-1, near_pot[2, 0]), (2, far_pot[0]), (-2, far_pot[1])):
        sent_back.append(passed_along(values, "band", -move))
    own_moves = table[MOVES : MOVES + local_domains]
    own_potential = jnp.zeros((local_domains, points), jnp.float32)
    for move, values in zip(SLOT_MOVES, sent_back):
        own_potential = jnp.where((own_moves == move)[:, None], values[None, :], own_potential)
    return density, ham, own_potential


def solution(mesh):
    placed = (P(("band", "grid"), None, None, None), P(), P(), P(("band", "grid"), None, None))
    return jax.shard_map(
        whole_step,
        mesh=mesh,
        in_specs=placed,
        out_specs=(
            P(("band", "grid"), None, None, None),
            P(("band", "grid"), None, None, None),
            P(("band", "grid"), None),
        ),
        check_vma=False,
    )
```

```python
import functools

import jax
import jax.numpy as jnp
from jax import lax
from jax.experimental import pallas as pl
from jax.experimental.pallas import tpu as pltpu
from jax.sharding import PartitionSpec as P


DBLK = 5
ITERS = 4
BS = 256
TILE = 256
SLOT_MOVES = (0, 1, -1, 2, -2)
OWN_PLACE, STARTS, COUNTS, MOVES, TABLE = 0, 1, 6, 11, 16

NN = (((1,), (0,)), ((), ()))
NT = (((1,), (1,)), ((), ()))
TN = (((0,), (0,)), ((), ()))


def passed_along(x, axis, by):
    count = lax.axis_size(axis)
    pairs = [(i, i + by) for i in range(count) if 0 <= i + by < count]
    return lax.ppermute(x, axis, pairs)


DETOUR = ((0, 2), (1, 4))


def detour_out(band_count, grid_count):
    last = grid_count - 1
    pairs = []
    for b in range(band_count):
        for g, via in DETOUR:
            if b + 1 < band_count:
                pairs.append((b * grid_count + g, (b + 1) * grid_count + via))
            if b > 0:
                pairs.append((b * grid_count + last - g, (b - 1) * grid_count + last - via))
    return pairs


def detour_back(band_count, grid_count):
    last = grid_count - 1
    pairs = []
    for b in range(band_count):
        for g, via in DETOUR:
            pairs.append((b * grid_count + via, b * grid_count + g))
            pairs.append((b * grid_count + last - via, b * grid_count + last - g))
    return pairs


def dot32(a, b, dims):
    return lax.dot_general(a, b, dims, preferred_element_type=jnp.float32)


def edge_blocks(rows):
    return ((0, 0), (0, 1), (1, 0), (rows - 2, 2), (rows - 1, 1), (rows - 1, 2))


def local_kernel(
    choice_ref, x_ref, edge_ref, narrow_ref, down_ref, up_ref, x_out, narrow_out, ext
):
    rows = narrow_ref.shape[0]
    edges = edge_blocks(rows)
    none = jnp.zeros((BS, BS), jnp.bfloat16)
    for r in (0, 1, rows + 2, rows + 3):
        for q in range(3):
            ext[r, q] = none
    for r in range(rows):
        for q in range(3):
            if (r, q) in edges:
                place = edges.index((r, q))
                ext[r + 2, q] = down_ref[place] if place < 3 else up_ref[place - 3]
            else:
                ext[r + 2, q] = narrow_ref[r, q]
    twice = choice_ref[0] == 1

    @pl.loop(0, rows)
    def _(row):
        i = row + 2
        here = [ext[i, q] for q in range(3)]
        up1, up0 = ext[i - 1, 1], ext[i - 1, 2]
        upup = ext[i - 2, 2]
        dn1, dn0 = ext[i + 1, 1], ext[i + 1, 0]
        dd = ext[i + 2, 0]
        diag = (
            dot32(here[0], here[0], NT)
            + dot32(here[1], here[1], NT)
            + dot32(here[2], here[2], NT)
            + dot32(dn1, dn1, TN)
            + dot32(dd, dd, TN)
        )
        near = (
            dot32(here[0], up1, NT)
            + dot32(here[1], up0, NN)
            + dot32(here[2], here[1], NN)
            + dot32(dn1, dn0, TN)
        )
        far = dot32(here[0], upup, NN) + dot32(here[1], up1, NN) + dot32(here[2], here[0], NN)
        for q, squared in ((0, far), (1, near), (2, diag)):
            new = jnp.where(twice, 2.0 * x_ref[row, q] - squared, squared)
            x_out[row, q] = new
            narrow_out[row, q] = new.astype(jnp.bfloat16)

    @pl.when(twice)
    def _():
        for place, (r, q) in enumerate(edges):
            x_out[r, q] += 2.0 * (edge_ref[place] - x_ref[r, q])


def local_step(choice, x, edge, narrow, down, up):
    rows = x.shape[0]
    vmem = pl.BlockSpec(memory_space=pltpu.VMEM)
    return pl.pallas_call(
        local_kernel,
        in_specs=[pl.BlockSpec(memory_space=pltpu.SMEM)] + [vmem] * 5,
        out_specs=[vmem, vmem],
        out_shape=[
            jax.ShapeDtypeStruct(x.shape, jnp.float32),
            jax.ShapeDtypeStruct(x.shape, jnp.bfloat16),
        ],
        scratch_shapes=[pltpu.VMEM((rows + 4, 3, BS, BS), jnp.bfloat16)],
        compiler_params=pltpu.CompilerParams(vmem_limit_bytes=8 << 20),
        cost_estimate=pl.CostEstimate(
            flops=rows * 12 * 2 * BS**3, bytes_accessed=x.size * 4, transcendentals=0
        ),
        name="local_step",
    )(choice, x, edge, narrow, down, up)


def border_kernel(
    choice_ref, before_ref, top_ref, bottom_ref, x_ref, edge_out, down_out, up_out
):
    rows = x_ref.shape[0]
    sign = jnp.where(choice_ref[0] == 1, -1.0, 1.0)
    x00, x01, x10 = before_ref[0], before_ref[1], before_ref[2]
    t_far, t_mid, t_near = top_ref[0], top_ref[1], top_ref[2]
    b_far, b_near, b_last = bottom_ref[0], bottom_ref[1], bottom_ref[2]
    added = (
        lambda: dot32(x00, t_far, NN) + dot32(x01, t_mid, NN),
        lambda: dot32(x00, t_mid, NT) + dot32(x01, t_near, NN),
        lambda: dot32(x10, t_near, NN),
        lambda: dot32(b_far, b_far, TN),
        lambda: dot32(b_near, b_far, TN),
        lambda: dot32(b_near, b_near, TN) + dot32(b_last, b_last, TN),
    )
    for place, (r, q) in enumerate(edge_blocks(rows)):
        new = x_ref[r, q] + sign * added[place]()
        edge_out[place] = new
        if place < 3:
            down_out[place] = new.astype(jnp.bfloat16)
        else:
            up_out[place - 3] = new.astype(jnp.bfloat16)


def border_step(choice, before, top, bottom, x):
    vmem = pl.BlockSpec(memory_space=pltpu.VMEM)
    edge = jax.ShapeDtypeStruct(top.shape, jnp.bfloat16)
    return pl.pallas_call(
        border_kernel,
        in_specs=[pl.BlockSpec(memory_space=pltpu.SMEM)] + [vmem] * 4,
        out_specs=[vmem] * 3,
        out_shape=[jax.ShapeDtypeStruct((6, BS, BS), jnp.float32), edge, edge],
        compiler_params=pltpu.CompilerParams(vmem_limit_bytes=4 << 20),
        cost_estimate=pl.CostEstimate(
            flops=9 * 2 * BS**3, bytes_accessed=x.size, transcendentals=0
        ),
        name="border_step",
    )(choice, before, top, bottom, x)


def density_kernel(x_ref, edge_ref, out, sems):
    rows = x_ref.shape[0]
    edges = edge_blocks(rows)
    copies = []
    for r in range(rows):
        for q in range(3):
            source = edge_ref.at[edges.index((r, q))] if (r, q) in edges else x_ref.at[r, q]
            copies.append(pltpu.make_async_copy(source, out.at[r, q], sems.at[r * 3 + q]))
    for copy in copies:
        copy.start()
    for copy in copies:
        copy.wait()


def density_step(x, edge):
    vmem = pl.BlockSpec(memory_space=pltpu.VMEM)
    return pl.pallas_call(
        density_kernel,
        in_specs=[vmem, vmem],
        out_specs=pl.BlockSpec(memory_space=pltpu.HBM),
        out_shape=pltpu.HBM(x.shape, jnp.float32),
        scratch_shapes=[pltpu.SemaphoreType.DMA((x.shape[0] * 3,))],
        compiler_params=pltpu.CompilerParams(vmem_limit_bytes=8 << 20),
        cost_estimate=pl.CostEstimate(flops=0, bytes_accessed=x.size * 4, transcendentals=0),
        name="density_step",
    )(x, edge)


def plan_kernel(moves, geometry, blocks_ref, basis_ref, *refs):
    *outs, table_ref, buf, in_sems, out_sems = refs
    rows, band_count, grid_count = geometry
    local = basis_ref.shape[0]
    band = lax.axis_index("band")
    grid = lax.axis_index("grid")
    device = band * grid_count + grid
    own_moves = []
    for d in range(local):
        first = blocks_ref[0, device * local + d]
        own_moves.append(first // (rows * grid_count) - band)

    def place_of(move):
        place = jnp.int32(0)
        for d in range(local):
            place = jnp.where(own_moves[d] == move, d, place)
        return place

    for n, move in enumerate(moves):
        pltpu.make_async_copy(basis_ref.at[place_of(move)], buf.at[n], in_sems.at[n]).start()
    table_ref[OWN_PLACE] = place_of(0)
    for slot, move in enumerate(SLOT_MOVES):
        source = band - move
        live = (source >= 0) & (source < band_count)
        source = jnp.clip(source, 0, band_count - 1) * grid_count + grid
        start = jnp.int32(0)
        count = jnp.int32(0)
        for d in range(local):
            first = blocks_ref[0, source * local + d]
            match = live & (first // rows == device)
            blocks = jnp.int32(0)
            for k in range(DBLK):
                blocks += jnp.where(blocks_ref[k, source * local + d] >= 0, 1, 0)
            start = jnp.where(match, first - device * rows, start)
            count = jnp.where(match, blocks, count)
        table_ref[STARTS + slot] = start
        table_ref[COUNTS + slot] = count
    for d in range(local):
        table_ref[MOVES + d] = own_moves[d]
    for n, move in enumerate(moves):
        pltpu.make_async_copy(basis_ref.at[place_of(move)], buf.at[n], in_sems.at[n]).wait()
        pltpu.make_async_copy(buf.at[n], outs[n], out_sems.at[n]).start()
    for n, move in enumerate(moves):
        pltpu.make_async_copy(buf.at[n], outs[n], out_sems.at[n]).wait()


def plan_step(moves, blocks, basis, rows, band_count, grid_count):
    any_space = pl.BlockSpec(memory_space=pl.ANY)
    smem = pl.BlockSpec(memory_space=pltpu.SMEM)
    one = jax.ShapeDtypeStruct(basis.shape[1:], basis.dtype)
    return pl.pallas_call(
        functools.partial(plan_kernel, moves, (rows, band_count, grid_count)),
        in_specs=[smem, pl.BlockSpec(memory_space=pltpu.HBM)],
        out_specs=[any_space] * len(moves) + [smem],
        out_shape=[one] * len(moves) + [jax.ShapeDtypeStruct((TABLE,), jnp.int32)],
        scratch_shapes=[
            pltpu.VMEM((len(moves),) + basis.shape[1:], basis.dtype),
            pltpu.SemaphoreType.DMA((len(moves),)),
            pltpu.SemaphoreType.DMA((len(moves),)),
        ],
        compiler_params=pltpu.CompilerParams(vmem_limit_bytes=16 << 20),
        name="plan_step",
    )(blocks, basis)


def pick_kernel(moves, cuts, table_ref, basis_ref, *refs):
    *outs, buf, in_sems, out_sems = refs
    local = basis_ref.shape[0]

    def place_of(move):
        place = jnp.int32(0)
        for d in range(local):
            place = jnp.where(table_ref[MOVES + d] == move, d, place)
        return place

    def load(n):
        return pltpu.make_async_copy(basis_ref.at[place_of(moves[n])], buf.at[n], in_sems.at[n])

    def stores(n):
        return [
            pltpu.make_async_copy(
                buf.at[n, pl.ds(low, high - low)],
                outs[n * len(cuts) + c],
                out_sems.at[n * len(cuts) + c],
            )
            for c, (low, high) in enumerate(cuts)
        ]

    for n in range(len(moves)):
        load(n).start()
    for n in range(len(moves)):
        load(n).wait()
        for copy in stores(n):
            copy.start()
    for n in range(len(moves)):
        for copy in stores(n):
            copy.wait()


def pick_step(moves, cuts, table, basis):
    any_space = pl.BlockSpec(memory_space=pl.ANY)
    smem = pl.BlockSpec(memory_space=pltpu.SMEM)
    width = basis.shape[2]
    outs = [jax.ShapeDtypeStruct((high - low, width), basis.dtype) for low, high in cuts]
    return pl.pallas_call(
        functools.partial(pick_kernel, moves, cuts),
        in_specs=[smem, pl.BlockSpec(memory_space=pltpu.HBM)],
        out_specs=[any_space] * (len(moves) * len(cuts)),
        out_shape=outs * len(moves),
        scratch_shapes=[
            pltpu.VMEM((len(moves),) + basis.shape[1:], basis.dtype),
            pltpu.SemaphoreType.DMA((len(moves),)),
            pltpu.SemaphoreType.DMA((len(moves) * len(cuts),)),
        ],
        compiler_params=pltpu.CompilerParams(vmem_limit_bytes=16 << 20),
        name="pick_step",
    )(table, basis)


def fill_stack(tile_refs, stack):
    main, down, up = tile_refs
    rows = main.shape[0]
    edges = edge_blocks(rows)

    def tile(r, q):
        if (r, q) not in edges:
            return main[r, q]
        place = edges.index((r, q))
        return down[place] if place < 3 else up[place - 3]

    for r in range(rows):
        stack[r, 0:BS] = tile(r, 2)
        for gap in (1, 2):
            where = pl.ds(gap * BS, BS)
            if r + gap < rows:
                stack[r, where] = tile(r + gap, 2 - gap) * 2
            else:
                stack[r, where] = jnp.zeros((BS, BS), jnp.bfloat16)


def blank_tail(phi, slot, blocks):
    for k in range(2, DBLK):

        @pl.when(k >= blocks)
        def _():
            phi[slot, :, k * BS : (k + 1) * BS] = jnp.zeros((phi.shape[1], BS), jnp.bfloat16)


def potential_of_slot(phi, slot, first, stack, pot_out, psi_at, factor):
    points = phi.shape[1]
    rows = stack.shape[0]

    @pl.loop(0, points // TILE)
    def _(step):
        here = pl.ds(pl.multiple_of(step * TILE, TILE), TILE)
        total = jnp.zeros((TILE, BS), jnp.float32)
        for j in range(DBLK):
            last = min(j + 3, DBLK)
            row = jnp.minimum(first + j, rows - 1)
            applied = dot32(phi[slot, here, j * BS : last * BS], stack[row, 0 : (last - j) * BS], NN)
            total += applied * phi[slot, here, j * BS : (j + 1) * BS].astype(jnp.float32)
        potential = jnp.tanh(jnp.sum(total, axis=1, keepdims=True))
        spread = jnp.transpose(jnp.broadcast_to(potential, (TILE, 128)))
        pot_out[slot, :, here] = spread[0:1]
        scale = factor * potential
        psi_at(here)[...] = (scale * phi[slot, here, :].astype(jnp.float32)).astype(jnp.bfloat16)


def add_blocks(ham, psi, phi, slot, first, blocks):
    for k in range(DBLK):

        @pl.when(k < blocks)
        def _():
            low = max(0, k - 2)
            piece = dot32(psi[:, k * BS : (k + 1) * BS], phi[slot, :, low * BS : (k + 1) * BS], TN)
            for j in range(low, k + 1):
                ham[first + k, 2 - (k - j)] += piece[:, (j - low) * BS : (j - low + 1) * BS]


def domain_kernel(slots, has_base, factor, table_ref, main_ref, down_ref, up_ref, *refs):
    refs = list(refs)
    base_ref = refs.pop(0) if has_base else None
    basis_refs = [refs.pop(0) for _ in slots]
    ham, pot_out, phi, psi, stack, sems = refs

    def fetch(n):
        source = basis_refs[n]
        if len(source.shape) == 3:
            source = source.at[table_ref[OWN_PLACE]]
        return pltpu.make_async_copy(source, phi.at[n], sems.at[n])

    for n in range(len(slots)):
        fetch(n).start()
    for r in range(ham.shape[0]):
        ham[r] = base_ref[r] if has_base else jnp.zeros_like(ham[r])
    fill_stack((main_ref, down_ref, up_ref), stack)
    pot_out[...] = jnp.zeros_like(pot_out)
    for n in range(len(slots)):
        fetch(n).wait()

    @pl.loop(0, len(slots))
    def _(n):
        first = table_ref[STARTS + slots[0] + n]
        blocks = table_ref[COUNTS + slots[0] + n]

        @pl.when(blocks > 0)
        def _():
            blank_tail(phi, n, blocks)
            potential_of_slot(phi, n, first, stack, pot_out, lambda here: psi.at[here], factor)
            add_blocks(ham, psi, phi, n, first, blocks)


def domain_step(slots, table, tiles, base, arrays, factor):
    rows = tiles[0].shape[0]
    points, width = arrays[-1].shape[-2:]
    number = len(arrays)
    has_base = base is not None
    smem = pl.BlockSpec(memory_space=pltpu.SMEM)
    vmem = pl.BlockSpec(memory_space=pltpu.VMEM)
    hbm = pl.BlockSpec(memory_space=pl.ANY)
    operands = [table, *tiles] + ([base] if has_base else []) + list(arrays)
    return pl.pallas_call(
        functools.partial(domain_kernel, slots, has_base, factor),
        in_specs=[smem] + [vmem] * (3 + has_base) + [hbm] * number,
        out_specs=[vmem, vmem],
        out_shape=[
            jax.ShapeDtypeStruct((rows, 3, BS, BS), jnp.float32),
            jax.ShapeDtypeStruct((number, 1, points), jnp.float32),
        ],
        scratch_shapes=[
            pltpu.VMEM((number, points, width), jnp.bfloat16),
            pltpu.VMEM((points, width), jnp.bfloat16),
            pltpu.VMEM((rows, 3 * BS, BS), jnp.bfloat16),
            pltpu.SemaphoreType.DMA((number,)),
        ],
        compiler_params=pltpu.CompilerParams(vmem_limit_bytes=(8 << 20) + number * points * width * 2),
        cost_estimate=pl.CostEstimate(
            flops=number * 24 * 2 * points * BS * BS,
            bytes_accessed=number * points * width * 2 + rows * 3 * BS * BS * 6,
            transcendentals=number * points,
        ),
        name="domain_step",
    )(*operands)


def potential_kernel(slots, factor, table_ref, main_ref, down_ref, up_ref, *refs):
    *basis_refs, detour_ref = refs[: len(slots) + 1]
    psi_out, phi_out, pot_out, phi, stack = refs[len(slots) + 1 :]
    points, width = phi.shape[1:]
    pad = phi_out.shape[2] - width
    grid = lax.axis_index("grid")
    last = lax.axis_size("grid") - 1
    detoured = (grid <= 1, grid >= last - 1)
    fill_stack((main_ref, down_ref, up_ref), stack)
    pot_out[...] = jnp.zeros_like(pot_out)
    for n in range(len(slots)):

        @pl.when(detoured[n])
        def _():
            phi[n] = detour_ref[...]

        @pl.when(jnp.logical_not(detoured[n]))
        def _():
            phi[n] = basis_refs[n][...]

        phi_out[n, :, 0:pad] = jnp.zeros((points, pad), jnp.bfloat16)

    @pl.loop(0, len(slots))
    def _(n):
        first = table_ref[STARTS + slots[0] + n]
        blocks = table_ref[COUNTS + slots[0] + n]

        @pl.when(blocks > 0)
        def _():
            blank_tail(phi, n, blocks)
            phi_out[n, :, pad:] = phi[n]
            potential_of_slot(phi, n, first, stack, pot_out, lambda here: psi_out.at[n, here], factor)


def potential_step(slots, table, tiles, arrays, detour, factor):
    rows = tiles[0].shape[0]
    points, width = arrays[-1].shape
    number = len(arrays)
    smem = pl.BlockSpec(memory_space=pltpu.SMEM)
    vmem = pl.BlockSpec(memory_space=pltpu.VMEM)
    return pl.pallas_call(
        functools.partial(potential_kernel, slots, factor),
        in_specs=[smem] + [vmem] * (4 + number),
        out_specs=[vmem] * 3,
        out_shape=[
            jax.ShapeDtypeStruct((number, points, width), jnp.bfloat16),
            jax.ShapeDtypeStruct((number, points, width + 2 * BS), jnp.bfloat16),
            jax.ShapeDtypeStruct((number, 1, points), jnp.float32),
        ],
        scratch_shapes=[
            pltpu.VMEM((number, points, width), jnp.bfloat16),
            pltpu.VMEM((rows, 3 * BS, BS), jnp.bfloat16),
        ],
        compiler_params=pltpu.CompilerParams(vmem_limit_bytes=10 << 20),
        cost_estimate=pl.CostEstimate(
            flops=number * 12 * 2 * points * BS * BS,
            bytes_accessed=number * points * width * 4,
            transcendentals=number * points,
        ),
        name="potential_step",
    )(table, *tiles, *arrays, detour)


def block_kernel(slots, table_ref, psi_ref, phi_ref, base_ref, ham_out, ham, sems):
    rows = ham.shape[0]

    def send(r):
        return pltpu.make_async_copy(ham.at[r], ham_out.at[r], sems.at[r])

    for r in range(rows):
        ham[r] = base_ref[r]
        for n, slot in enumerate(slots):
            k = r - table_ref[STARTS + slot]
            blocks = table_ref[COUNTS + slot]

            @pl.when((k >= 0) & (k < blocks))
            def _():
                offset = pl.multiple_of(k * BS, BS)
                left = psi_ref[n, :, pl.ds(offset, BS)]
                piece = dot32(left, phi_ref[n, :, pl.ds(offset, 3 * BS)], TN)
                for q in range(3):
                    ham[r, q] += piece[:, q * BS : (q + 1) * BS]

        send(r).start()
    for r in range(rows):
        send(r).wait()


def block_step(slots, table, psi, phi, base):
    number, points, width = psi.shape
    rows = base.shape[0]
    smem = pl.BlockSpec(memory_space=pltpu.SMEM)
    vmem = pl.BlockSpec(memory_space=pltpu.VMEM)
    return pl.pallas_call(
        functools.partial(block_kernel, slots),
        in_specs=[smem, vmem, vmem, vmem],
        out_specs=pl.BlockSpec(memory_space=pltpu.HBM),
        out_shape=pltpu.HBM(base.shape, jnp.float32),
        scratch_shapes=[
            pltpu.VMEM(base.shape, jnp.float32),
            pltpu.SemaphoreType.DMA((rows,)),
        ],
        compiler_params=pltpu.CompilerParams(vmem_limit_bytes=10 << 20),
        cost_estimate=pl.CostEstimate(
            flops=number * 12 * 2 * points * BS * BS,
            bytes_accessed=number * points * width * 4 + base.size * 8,
            transcendentals=0,
        ),
        name="block_step",
    )(table, psi, phi, base)


def whole_step(x_initial, sp2_choices, domain_blocks, basis_values):
    row_count = x_initial.shape[0]
    band_count = lax.axis_size("band")
    grid_count = lax.axis_size("grid")
    local_domains, points, width = basis_values.shape
    factor = width / points
    cuts = ((0, 512), (512, points))

    def orbitals(value, move):
        return passed_along(value, "band", move)

    basis_values = pltpu.with_memory_space_constraint(basis_values, pltpu.HBM)
    blocks = pltpu.with_memory_space_constraint(domain_blocks.T, pltpu.HBM)
    plus, minus, table = plan_step(
        (2, -2), blocks, basis_values, row_count, band_count, grid_count
    )
    halfway = [orbitals(plus, 1), orbitals(minus, -1)]
    plus, minus = pick_step((1, -1), ((0, points),), table, basis_values)
    near = [orbitals(plus, 1), orbitals(minus, -1)]
    far_a = [orbitals(halfway[n][: cuts[0][1]], 1 - 2 * n) for n in (0, 1)]
    rest = [halfway[n][cuts[1][0] :] for n in (0, 1)]
    turned = jnp.where(lax.axis_index("grid") < grid_count // 2, rest[0], rest[1])
    detour = lax.ppermute(turned, ("band", "grid"), detour_out(band_count, grid_count))
    far_b = []
    for n, skipped in ((0, (0, 1)), (1, (grid_count - 2, grid_count - 1))):
        move = 1 - 2 * n
        pairs = [
            (b * grid_count + g, (b + move) * grid_count + g)
            for b in range(band_count)
            for g in range(grid_count)
            if 0 <= b + move < band_count and g not in skipped
        ]
        far_b.append(lax.ppermute(rest[n], ("band", "grid"), pairs))
    detour = lax.ppermute(detour, ("band", "grid"), detour_back(band_count, grid_count))

    x = x_initial
    narrow = x.astype(jnp.bfloat16)
    upward = jnp.stack([narrow[-2, 2], narrow[-1, 1], narrow[-1, 2]])
    downward = jnp.stack([narrow[0, 0], narrow[0, 1], narrow[1, 0]])
    edge = jnp.stack([x[r, q] for r, q in edge_blocks(row_count)])
    for iteration in range(ITERS):
        choice = sp2_choices[iteration : iteration + 1]
        top = passed_along(upward, ("band", "grid"), 1)
        bottom = passed_along(downward, ("band", "grid"), -1)
        before = downward
        x, narrow = local_step(choice, x, edge, narrow, downward, upward)
        edge, downward, upward = border_step(choice, before, top, bottom, x)
    tiles = (narrow, downward, upward)
    density = density_step(x, edge)

    ham, near_pot = domain_step((0, 1, 2), table, tiles, None, [basis_values] + near, factor)
    ham, pot_a = domain_step((3, 4), table, tiles, ham, far_a, factor)
    psi_b, phi_b, pot_b = potential_step((3, 4), table, tiles, far_b, detour, factor)
    far_pot = [jnp.concatenate([pot_a[n, 0], pot_b[n, 0]]) for n in (0, 1)]
    ham = block_step((3, 4), table, psi_b, phi_b, ham)
    sent_back = [near_pot[0, 0]]
    for move, values in ((1, near_pot[1, 0]), (-1, near_pot[2, 0]), (2, far_pot[0]), (-2, far_pot[1])):
        sent_back.append(passed_along(values, "band", -move))
    own_moves = table[MOVES : MOVES + local_domains]
    own_potential = jnp.zeros((local_domains, points), jnp.float32)
    for move, values in zip(SLOT_MOVES, sent_back):
        own_potential = jnp.where((own_moves == move)[:, None], values[None, :], own_potential)
    return density, ham, own_potential


def solution(mesh):
    placed = (P(("band", "grid"), None, None, None), P(), P(), P(("band", "grid"), None, None))
    return jax.shard_map(
        whole_step,
        mesh=mesh,
        in_specs=placed,
        out_specs=(
            P(("band", "grid"), None, None, None),
            P(("band", "grid"), None, None, None),
            P(("band", "grid"), None),
        ),
        check_vma=False,
    )
```

```python
import functools

import jax
import jax.numpy as jnp
from jax import lax
from jax.experimental import pallas as pl
from jax.experimental.pallas import tpu as pltpu
from jax.sharding import PartitionSpec as P


DBLK = 5
RB = 5
ITERS = 4
BS = 256
TILE = 256
SLOT_MOVES = (0, 1, -1, 2, -2)
OWN_PLACE, STARTS, COUNTS, MOVES, TABLE = 0, 1, 6, 11, 16

NN = (((1,), (0,)), ((), ()))
NT = (((1,), (1,)), ((), ()))
TN = (((0,), (0,)), ((), ()))


def passed_along(x, axis, by):
    count = lax.axis_size(axis)
    pairs = [(i, i + by) for i in range(count) if 0 <= i + by < count]
    return lax.ppermute(x, axis, pairs)


DETOUR = ((0, 2), (1, 4))


def detour_out(band_count, grid_count):
    last = grid_count - 1
    pairs = []
    for b in range(band_count):
        for g, via in DETOUR:
            if b + 1 < band_count:
                pairs.append((b * grid_count + g, (b + 1) * grid_count + via))
            if b > 0:
                pairs.append((b * grid_count + last - g, (b - 1) * grid_count + last - via))
    return pairs


def detour_back(band_count, grid_count):
    last = grid_count - 1
    pairs = []
    for b in range(band_count):
        for g, via in DETOUR:
            pairs.append((b * grid_count + via, b * grid_count + g))
            pairs.append((b * grid_count + last - via, b * grid_count + last - g))
    return pairs


def dot32(a, b, dims):
    return lax.dot_general(a, b, dims, preferred_element_type=jnp.float32)


def edge_blocks(rows):
    return ((0, 0), (0, 1), (1, 0), (rows - 2, 2), (rows - 1, 1), (rows - 1, 2))


def local_kernel(
    choice_ref, x_ref, edge_ref, narrow_ref, down_ref, up_ref, x_out, narrow_out, ext
):
    rows = narrow_ref.shape[0]
    edges = edge_blocks(rows)
    none = jnp.zeros((BS, BS), jnp.bfloat16)
    for r in (0, 1, rows + 2, rows + 3):
        for q in range(3):
            ext[r, q] = none
    for r in range(rows):
        for q in range(3):
            if (r, q) in edges:
                place = edges.index((r, q))
                ext[r + 2, q] = down_ref[place] if place < 3 else up_ref[place - 3]
            else:
                ext[r + 2, q] = narrow_ref[r, q]
    twice = choice_ref[0] == 1

    @pl.loop(0, rows)
    def _(row):
        i = row + 2
        here = [ext[i, q] for q in range(3)]
        up1, up0 = ext[i - 1, 1], ext[i - 1, 2]
        upup = ext[i - 2, 2]
        dn1, dn0 = ext[i + 1, 1], ext[i + 1, 0]
        dd = ext[i + 2, 0]
        diag = (
            dot32(here[0], here[0], NT)
            + dot32(here[1], here[1], NT)
            + dot32(here[2], here[2], NT)
            + dot32(dn1, dn1, TN)
            + dot32(dd, dd, TN)
        )
        near = (
            dot32(here[0], up1, NT)
            + dot32(here[1], up0, NN)
            + dot32(here[2], here[1], NN)
            + dot32(dn1, dn0, TN)
        )
        far = dot32(here[0], upup, NN) + dot32(here[1], up1, NN) + dot32(here[2], here[0], NN)
        for q, squared in ((0, far), (1, near), (2, diag)):
            new = jnp.where(twice, 2.0 * x_ref[row, q] - squared, squared)
            x_out[row, q] = new
            narrow_out[row, q] = new.astype(jnp.bfloat16)

    @pl.when(twice)
    def _():
        for place, (r, q) in enumerate(edges):
            x_out[r, q] += 2.0 * (edge_ref[place] - x_ref[r, q])


def local_step(choice, x, edge, narrow, down, up):
    rows = x.shape[0]
    vmem = pl.BlockSpec(memory_space=pltpu.VMEM)
    return pl.pallas_call(
        local_kernel,
        in_specs=[pl.BlockSpec(memory_space=pltpu.SMEM)] + [vmem] * 5,
        out_specs=[vmem, vmem],
        out_shape=[
            jax.ShapeDtypeStruct(x.shape, jnp.float32),
            jax.ShapeDtypeStruct(x.shape, jnp.bfloat16),
        ],
        scratch_shapes=[pltpu.VMEM((rows + 4, 3, BS, BS), jnp.bfloat16)],
        compiler_params=pltpu.CompilerParams(vmem_limit_bytes=8 << 20),
        cost_estimate=pl.CostEstimate(
            flops=rows * 12 * 2 * BS**3, bytes_accessed=x.size * 4, transcendentals=0
        ),
        name="local_step",
    )(choice, x, edge, narrow, down, up)


def border_kernel(
    choice_ref, before_ref, top_ref, bottom_ref, x_ref, edge_out, down_out, up_out
):
    rows = x_ref.shape[0]
    sign = jnp.where(choice_ref[0] == 1, -1.0, 1.0)
    x00, x01, x10 = before_ref[0], before_ref[1], before_ref[2]
    t_far, t_mid, t_near = top_ref[0], top_ref[1], top_ref[2]
    b_far, b_near, b_last = bottom_ref[0], bottom_ref[1], bottom_ref[2]
    added = (
        lambda: dot32(x00, t_far, NN) + dot32(x01, t_mid, NN),
        lambda: dot32(x00, t_mid, NT) + dot32(x01, t_near, NN),
        lambda: dot32(x10, t_near, NN),
        lambda: dot32(b_far, b_far, TN),
        lambda: dot32(b_near, b_far, TN),
        lambda: dot32(b_near, b_near, TN) + dot32(b_last, b_last, TN),
    )
    for place, (r, q) in enumerate(edge_blocks(rows)):
        new = x_ref[r, q] + sign * added[place]()
        edge_out[place] = new
        if place < 3:
            down_out[place] = new.astype(jnp.bfloat16)
        else:
            up_out[place - 3] = new.astype(jnp.bfloat16)


def border_step(choice, before, top, bottom, x):
    vmem = pl.BlockSpec(memory_space=pltpu.VMEM)
    edge = jax.ShapeDtypeStruct(top.shape, jnp.bfloat16)
    return pl.pallas_call(
        border_kernel,
        in_specs=[pl.BlockSpec(memory_space=pltpu.SMEM)] + [vmem] * 4,
        out_specs=[vmem] * 3,
        out_shape=[jax.ShapeDtypeStruct((6, BS, BS), jnp.float32), edge, edge],
        compiler_params=pltpu.CompilerParams(vmem_limit_bytes=4 << 20),
        cost_estimate=pl.CostEstimate(
            flops=9 * 2 * BS**3, bytes_accessed=x.size, transcendentals=0
        ),
        name="border_step",
    )(choice, before, top, bottom, x)


def density_kernel(x_ref, edge_ref, out, sems):
    rows = x_ref.shape[0]
    edges = edge_blocks(rows)
    copies = []
    for r in range(rows):
        for q in range(3):
            source = edge_ref.at[edges.index((r, q))] if (r, q) in edges else x_ref.at[r, q]
            copies.append(pltpu.make_async_copy(source, out.at[r, q], sems.at[r * 3 + q]))
    for copy in copies:
        copy.start()
    for copy in copies:
        copy.wait()


def density_step(x, edge):
    vmem = pl.BlockSpec(memory_space=pltpu.VMEM)
    return pl.pallas_call(
        density_kernel,
        in_specs=[vmem, vmem],
        out_specs=pl.BlockSpec(memory_space=pltpu.HBM),
        out_shape=pltpu.HBM(x.shape, jnp.float32),
        scratch_shapes=[pltpu.SemaphoreType.DMA((x.shape[0] * 3,))],
        compiler_params=pltpu.CompilerParams(vmem_limit_bytes=8 << 20),
        cost_estimate=pl.CostEstimate(flops=0, bytes_accessed=x.size * 4, transcendentals=0),
        name="density_step",
    )(x, edge)


def plan_kernel(moves, geometry, blocks_ref, basis_ref, *refs):
    *outs, table_ref, buf, in_sems, out_sems = refs
    rows, band_count, grid_count = geometry
    local = basis_ref.shape[0]
    band = lax.axis_index("band")
    grid = lax.axis_index("grid")
    device = band * grid_count + grid
    own_moves = []
    for d in range(local):
        first = blocks_ref[0, device * local + d]
        own_moves.append(first // (rows * grid_count) - band)

    def place_of(move):
        place = jnp.int32(0)
        for d in range(local):
            place = jnp.where(own_moves[d] == move, d, place)
        return place

    for n, move in enumerate(moves):
        pltpu.make_async_copy(basis_ref.at[place_of(move)], buf.at[n], in_sems.at[n]).start()
    table_ref[OWN_PLACE] = place_of(0)
    for slot, move in enumerate(SLOT_MOVES):
        source = band - move
        live = (source >= 0) & (source < band_count)
        source = jnp.clip(source, 0, band_count - 1) * grid_count + grid
        start = jnp.int32(0)
        count = jnp.int32(0)
        for d in range(local):
            first = blocks_ref[0, source * local + d]
            match = live & (first // rows == device)
            blocks = jnp.int32(0)
            for k in range(DBLK):
                blocks += jnp.where(blocks_ref[k, source * local + d] >= 0, 1, 0)
            start = jnp.where(match, first - device * rows, start)
            count = jnp.where(match, blocks, count)
        table_ref[STARTS + slot] = start
        table_ref[COUNTS + slot] = count
    for d in range(local):
        table_ref[MOVES + d] = own_moves[d]
    for n, move in enumerate(moves):
        pltpu.make_async_copy(basis_ref.at[place_of(move)], buf.at[n], in_sems.at[n]).wait()
        pltpu.make_async_copy(buf.at[n], outs[n], out_sems.at[n]).start()
    for n, move in enumerate(moves):
        pltpu.make_async_copy(buf.at[n], outs[n], out_sems.at[n]).wait()


def plan_step(moves, blocks, basis, rows, band_count, grid_count):
    any_space = pl.BlockSpec(memory_space=pl.ANY)
    smem = pl.BlockSpec(memory_space=pltpu.SMEM)
    one = jax.ShapeDtypeStruct(basis.shape[1:], basis.dtype)
    return pl.pallas_call(
        functools.partial(plan_kernel, moves, (rows, band_count, grid_count)),
        in_specs=[smem, pl.BlockSpec(memory_space=pltpu.HBM)],
        out_specs=[any_space] * len(moves) + [smem],
        out_shape=[one] * len(moves) + [jax.ShapeDtypeStruct((TABLE,), jnp.int32)],
        scratch_shapes=[
            pltpu.VMEM((len(moves),) + basis.shape[1:], basis.dtype),
            pltpu.SemaphoreType.DMA((len(moves),)),
            pltpu.SemaphoreType.DMA((len(moves),)),
        ],
        compiler_params=pltpu.CompilerParams(vmem_limit_bytes=16 << 20),
        name="plan_step",
    )(blocks, basis)


def pick_kernel(moves, cuts, table_ref, basis_ref, *refs):
    *outs, buf, in_sems, out_sems = refs
    local = basis_ref.shape[0]

    def place_of(move):
        place = jnp.int32(0)
        for d in range(local):
            place = jnp.where(table_ref[MOVES + d] == move, d, place)
        return place

    def load(n):
        return pltpu.make_async_copy(basis_ref.at[place_of(moves[n])], buf.at[n], in_sems.at[n])

    def stores(n):
        return [
            pltpu.make_async_copy(
                buf.at[n, pl.ds(low, high - low)],
                outs[n * len(cuts) + c],
                out_sems.at[n * len(cuts) + c],
            )
            for c, (low, high) in enumerate(cuts)
        ]

    for n in range(len(moves)):
        load(n).start()
    for n in range(len(moves)):
        load(n).wait()
        for copy in stores(n):
            copy.start()
    for n in range(len(moves)):
        for copy in stores(n):
            copy.wait()


def pick_step(moves, cuts, table, basis):
    any_space = pl.BlockSpec(memory_space=pl.ANY)
    smem = pl.BlockSpec(memory_space=pltpu.SMEM)
    width = basis.shape[2]
    outs = [jax.ShapeDtypeStruct((high - low, width), basis.dtype) for low, high in cuts]
    return pl.pallas_call(
        functools.partial(pick_kernel, moves, cuts),
        in_specs=[smem, pl.BlockSpec(memory_space=pltpu.HBM)],
        out_specs=[any_space] * (len(moves) * len(cuts)),
        out_shape=outs * len(moves),
        scratch_shapes=[
            pltpu.VMEM((len(moves),) + basis.shape[1:], basis.dtype),
            pltpu.SemaphoreType.DMA((len(moves),)),
            pltpu.SemaphoreType.DMA((len(moves) * len(cuts),)),
        ],
        compiler_params=pltpu.CompilerParams(vmem_limit_bytes=16 << 20),
        name="pick_step",
    )(table, basis)


def fill_stack(tile_refs, stack):
    main, down, up = tile_refs
    rows = main.shape[0]
    edges = edge_blocks(rows)

    def tile(r, q):
        if (r, q) not in edges:
            return main[r, q]
        place = edges.index((r, q))
        return down[place] if place < 3 else up[place - 3]

    for r in range(rows):
        stack[r, 0:BS] = tile(r, 2)
        for gap in (1, 2):
            where = pl.ds(gap * BS, BS)
            if r + gap < rows:
                stack[r, where] = tile(r + gap, 2 - gap) * 2
            else:
                stack[r, where] = jnp.zeros((BS, BS), jnp.bfloat16)


def blank_tail(phi, slot, blocks):
    for k in range(2, DBLK):

        @pl.when(k >= blocks)
        def _():
            phi[slot, :, k * BS : (k + 1) * BS] = jnp.zeros((phi.shape[1], BS), jnp.bfloat16)


def potential_of_slot(phi, slot, first, stack, pot_out, psi_at, factor):
    points = phi.shape[1]
    rows = stack.shape[0]

    @pl.loop(0, points // TILE)
    def _(step):
        here = pl.ds(pl.multiple_of(step * TILE, TILE), TILE)
        total = jnp.zeros((TILE, BS), jnp.float32)
        for j in range(DBLK):
            last = min(j + 3, DBLK)
            row = jnp.minimum(first + j, rows - 1)
            applied = dot32(phi[slot, here, j * BS : last * BS], stack[row, 0 : (last - j) * BS], NN)
            total += applied * phi[slot, here, j * BS : (j + 1) * BS].astype(jnp.float32)
        potential = jnp.tanh(jnp.sum(total, axis=1, keepdims=True))
        spread = jnp.transpose(jnp.broadcast_to(potential, (TILE, 128)))
        pot_out[slot, :, here] = spread[0:1]
        scale = factor * potential
        psi_at(here)[...] = (scale * phi[slot, here, :].astype(jnp.float32)).astype(jnp.bfloat16)


def add_blocks(ham, psi, phi, slot, first):
    for k in range(DBLK):
        row = jnp.minimum(first + k, ham.shape[0] - 1)
        low = max(0, k - 2)
        piece = dot32(psi[:, k * BS : (k + 1) * BS], phi[slot, :, low * BS : (k + 1) * BS], TN)
        for j in range(low, k + 1):
            ham[row, 2 - (k - j)] += piece[:, (j - low) * BS : (j - low + 1) * BS]


def domain_kernel(slots, has_base, factor, table_ref, *refs):
    refs = list(refs)
    if has_base:
        base_ref, stack = refs.pop(0), refs.pop(0)
    else:
        tile_refs = [refs.pop(0) for _ in range(3)]
        stack = refs.pop(len(slots) + 2)
    basis_refs = [refs.pop(0) for _ in slots]
    ham, pot_out, phi, psi, sems = refs

    def fetch(n):
        source = basis_refs[n]
        if len(source.shape) == 3:
            source = source.at[table_ref[OWN_PLACE]]
        return pltpu.make_async_copy(source, phi.at[n], sems.at[n])

    for n in range(len(slots)):
        fetch(n).start()
    for r in range(ham.shape[0]):
        ham[r] = base_ref[r] if has_base else jnp.zeros_like(ham[r])
    if not has_base:
        fill_stack(tile_refs, stack)
    pot_out[...] = jnp.zeros_like(pot_out)
    for n in range(len(slots)):
        fetch(n).wait()

    @pl.loop(0, len(slots))
    def _(n):
        first = table_ref[STARTS + slots[0] + n]
        blocks = table_ref[COUNTS + slots[0] + n]

        @pl.when(blocks > 0)
        def _():
            blank_tail(phi, n, blocks)
            potential_of_slot(phi, n, first, stack, pot_out, lambda here: psi.at[here], factor)
            add_blocks(ham, psi, phi, n, first)


def domain_step(slots, table, tiles, base, arrays, factor):
    rows = RB
    points, width = arrays[-1].shape[-2:]
    number = len(arrays)
    has_base = base is not None
    smem = pl.BlockSpec(memory_space=pltpu.SMEM)
    vmem = pl.BlockSpec(memory_space=pltpu.VMEM)
    hbm = pl.BlockSpec(memory_space=pl.ANY)
    fixed = base if has_base else tiles
    outs = [
        jax.ShapeDtypeStruct((rows, 3, BS, BS), jnp.float32),
        jax.ShapeDtypeStruct((number, 1, points), jnp.float32),
    ]
    if not has_base:
        outs.append(jax.ShapeDtypeStruct((rows, 3 * BS, BS), jnp.bfloat16))
    return pl.pallas_call(
        functools.partial(domain_kernel, slots, has_base, factor),
        in_specs=[smem] + [vmem] * len(fixed) + [hbm] * number,
        out_specs=[vmem] * len(outs),
        out_shape=outs,
        scratch_shapes=[
            pltpu.VMEM((number, points, width), jnp.bfloat16),
            pltpu.VMEM((points, width), jnp.bfloat16),
            pltpu.SemaphoreType.DMA((number,)),
        ],
        compiler_params=pltpu.CompilerParams(
            vmem_limit_bytes=(8 << 20) + number * points * width * 2
        ),
        cost_estimate=pl.CostEstimate(
            flops=number * 24 * 2 * points * BS * BS,
            bytes_accessed=number * points * width * 2 + rows * 3 * BS * BS * 6,
            transcendentals=number * points,
        ),
        name="domain_step",
    )(table, *fixed, *arrays)


def potential_kernel(slots, factor, table_ref, stack, *refs):
    *basis_refs, detour_ref = refs[: len(slots) + 1]
    psi_out, phi_out, pot_out, phi = refs[len(slots) + 1 :]
    points, width = phi.shape[1:]
    pad = phi_out.shape[2] - width
    grid = lax.axis_index("grid")
    last = lax.axis_size("grid") - 1
    detoured = (grid <= 1, grid >= last - 1)
    pot_out[...] = jnp.zeros_like(pot_out)
    for n in range(len(slots)):

        @pl.when(detoured[n])
        def _():
            phi[n] = detour_ref[...]

        @pl.when(jnp.logical_not(detoured[n]))
        def _():
            phi[n] = basis_refs[n][...]

        phi_out[n, :, 0:pad] = jnp.zeros((points, pad), jnp.bfloat16)
        phi_out[n, :, pad:] = phi[n]
        psi_out[n, :, width:] = jnp.zeros((points, BS), jnp.bfloat16)

    @pl.loop(0, len(slots))
    def _(n):
        first = table_ref[STARTS + slots[0] + n]
        blocks = table_ref[COUNTS + slots[0] + n]

        @pl.when(blocks > 0)
        def _():
            blank_tail(phi, n, blocks)

            def psi_at(here):
                return psi_out.at[n, here, 0:width]

            potential_of_slot(phi, n, first, stack, pot_out, psi_at, factor)


def potential_step(slots, table, stack, arrays, detour, factor):
    points, width = arrays[-1].shape
    number = len(arrays)
    smem = pl.BlockSpec(memory_space=pltpu.SMEM)
    vmem = pl.BlockSpec(memory_space=pltpu.VMEM)
    return pl.pallas_call(
        functools.partial(potential_kernel, slots, factor),
        in_specs=[smem] + [vmem] * (2 + number),
        out_specs=[vmem] * 3,
        out_shape=[
            jax.ShapeDtypeStruct((number, points, width + BS), jnp.bfloat16),
            jax.ShapeDtypeStruct((number, points, width + 2 * BS), jnp.bfloat16),
            jax.ShapeDtypeStruct((number, 1, points), jnp.float32),
        ],
        scratch_shapes=[pltpu.VMEM((number, points, width), jnp.bfloat16)],
        compiler_params=pltpu.CompilerParams(vmem_limit_bytes=10 << 20),
        cost_estimate=pl.CostEstimate(
            flops=number * 12 * 2 * points * BS * BS,
            bytes_accessed=number * points * width * 4,
            transcendentals=number * points,
        ),
        name="potential_step",
    )(table, stack, *arrays, detour)


def block_kernel(slots, table_ref, psi_ref, phi_ref, base_ref, ham_out, ham, sems):
    rows = ham.shape[0]

    def send(r):
        return pltpu.make_async_copy(ham.at[r], ham_out.at[r], sems.at[r])

    for r in range(rows):
        total = None
        for n, slot in enumerate(slots):
            k = r - table_ref[STARTS + slot]
            held = (k >= 0) & (k < table_ref[COUNTS + slot])
            near = jnp.clip(k, 0, DBLK - 1)
            left = psi_ref[n, :, pl.ds(pl.multiple_of(jnp.where(held, near, DBLK) * BS, BS), BS)]
            right = phi_ref[n, :, pl.ds(pl.multiple_of(near * BS, BS), 3 * BS)]
            piece = dot32(left, right, TN)
            total = piece if total is None else total + piece
        for q in range(3):
            ham[r, q] = base_ref[r, q] + total[:, q * BS : (q + 1) * BS]
        send(r).start()
    for r in range(rows):
        send(r).wait()


def block_step(slots, table, psi, phi, base):
    number, points, width = psi.shape
    rows = base.shape[0]
    smem = pl.BlockSpec(memory_space=pltpu.SMEM)
    vmem = pl.BlockSpec(memory_space=pltpu.VMEM)
    return pl.pallas_call(
        functools.partial(block_kernel, slots),
        in_specs=[smem, vmem, vmem, vmem],
        out_specs=pl.BlockSpec(memory_space=pltpu.HBM),
        out_shape=pltpu.HBM(base.shape, jnp.float32),
        scratch_shapes=[
            pltpu.VMEM(base.shape, jnp.float32),
            pltpu.SemaphoreType.DMA((rows,)),
        ],
        compiler_params=pltpu.CompilerParams(vmem_limit_bytes=10 << 20),
        cost_estimate=pl.CostEstimate(
            flops=number * 12 * 2 * points * BS * BS,
            bytes_accessed=number * points * width * 4 + base.size * 8,
            transcendentals=0,
        ),
        name="block_step",
    )(table, psi, phi, base)


def whole_step(x_initial, sp2_choices, domain_blocks, basis_values):
    row_count = x_initial.shape[0]
    band_count = lax.axis_size("band")
    grid_count = lax.axis_size("grid")
    local_domains, points, width = basis_values.shape
    factor = width / points
    cuts = ((0, 512), (512, points))

    def orbitals(value, move):
        return passed_along(value, "band", move)

    basis_values = pltpu.with_memory_space_constraint(basis_values, pltpu.HBM)
    blocks = pltpu.with_memory_space_constraint(domain_blocks.T, pltpu.HBM)
    plus, minus, table = plan_step(
        (2, -2), blocks, basis_values, row_count, band_count, grid_count
    )
    halfway = [orbitals(plus, 1), orbitals(minus, -1)]
    plus, minus = pick_step((1, -1), ((0, points),), table, basis_values)
    near = [orbitals(plus, 1), orbitals(minus, -1)]
    far_a = [orbitals(halfway[n][: cuts[0][1]], 1 - 2 * n) for n in (0, 1)]
    rest = [halfway[n][cuts[1][0] :] for n in (0, 1)]
    turned = jnp.where(lax.axis_index("grid") < grid_count // 2, rest[0], rest[1])
    detour = lax.ppermute(turned, ("band", "grid"), detour_out(band_count, grid_count))
    far_b = []
    for n, skipped in ((0, (0, 1)), (1, (grid_count - 2, grid_count - 1))):
        move = 1 - 2 * n
        pairs = [
            (b * grid_count + g, (b + move) * grid_count + g)
            for b in range(band_count)
            for g in range(grid_count)
            if 0 <= b + move < band_count and g not in skipped
        ]
        far_b.append(lax.ppermute(rest[n], ("band", "grid"), pairs))
    detour = lax.ppermute(detour, ("band", "grid"), detour_back(band_count, grid_count))

    x = x_initial
    narrow = x.astype(jnp.bfloat16)
    upward = jnp.stack([narrow[-2, 2], narrow[-1, 1], narrow[-1, 2]])
    downward = jnp.stack([narrow[0, 0], narrow[0, 1], narrow[1, 0]])
    edge = jnp.stack([x[r, q] for r, q in edge_blocks(row_count)])
    for iteration in range(ITERS):
        choice = sp2_choices[iteration : iteration + 1]
        top = passed_along(upward, ("band", "grid"), 1)
        bottom = passed_along(downward, ("band", "grid"), -1)
        before = downward
        x, narrow = local_step(choice, x, edge, narrow, downward, upward)
        edge, downward, upward = border_step(choice, before, top, bottom, x)
    tiles = (narrow, downward, upward)
    density = density_step(x, edge)

    ham, near_pot, stack = domain_step((0, 1, 2), table, tiles, None, [basis_values] + near, factor)
    ham, pot_a = domain_step((3, 4), table, None, (ham, stack), far_a, factor)
    psi_b, phi_b, pot_b = potential_step((3, 4), table, stack, far_b, detour, factor)
    far_pot = [jnp.concatenate([pot_a[n, 0], pot_b[n, 0]]) for n in (0, 1)]
    ham = block_step((3, 4), table, psi_b, phi_b, ham)
    sent_back = [near_pot[0, 0]]
    for move, values in ((1, near_pot[1, 0]), (-1, near_pot[2, 0]), (2, far_pot[0]), (-2, far_pot[1])):
        sent_back.append(passed_along(values, "band", -move))
    own_moves = table[MOVES : MOVES + local_domains]
    own_potential = jnp.zeros((local_domains, points), jnp.float32)
    for move, values in zip(SLOT_MOVES, sent_back):
        own_potential = jnp.where((own_moves == move)[:, None], values[None, :], own_potential)
    return density, ham, own_potential


def solution(mesh):
    placed = (P(("band", "grid"), None, None, None), P(), P(), P(("band", "grid"), None, None))
    return jax.shard_map(
        whole_step,
        mesh=mesh,
        in_specs=placed,
        out_specs=(
            P(("band", "grid"), None, None, None),
            P(("band", "grid"), None, None, None),
            P(("band", "grid"), None),
        ),
        check_vma=False,
    )
```

```python
import functools

import jax
import jax.numpy as jnp
from jax import lax
from jax.experimental import pallas as pl
from jax.experimental.pallas import tpu as pltpu
from jax.sharding import PartitionSpec as P


DBLK = 5
RB = 5
ITERS = 4
BS = 256
TILE = 256
SLOT_MOVES = (0, 1, -1, 2, -2)
OWN_PLACE, STARTS, COUNTS, MOVES, TABLE = 0, 1, 6, 11, 16

NN = (((1,), (0,)), ((), ()))
NT = (((1,), (1,)), ((), ()))
TN = (((0,), (0,)), ((), ()))


def passed_along(x, axis, by):
    count = lax.axis_size(axis)
    pairs = [(i, i + by) for i in range(count) if 0 <= i + by < count]
    return lax.ppermute(x, axis, pairs)


DETOUR = ((0, 2), (1, 4))


def detour_out(band_count, grid_count):
    last = grid_count - 1
    pairs = []
    for b in range(band_count):
        for g, via in DETOUR:
            if b + 1 < band_count:
                pairs.append((b * grid_count + g, (b + 1) * grid_count + via))
            if b > 0:
                pairs.append((b * grid_count + last - g, (b - 1) * grid_count + last - via))
    return pairs


def detour_back(band_count, grid_count):
    last = grid_count - 1
    pairs = []
    for b in range(band_count):
        for g, via in DETOUR:
            pairs.append((b * grid_count + via, b * grid_count + g))
            pairs.append((b * grid_count + last - via, b * grid_count + last - g))
    return pairs


def dot32(a, b, dims):
    return lax.dot_general(a, b, dims, preferred_element_type=jnp.float32)


def edge_blocks(rows):
    return ((0, 0), (0, 1), (1, 0), (rows - 2, 2), (rows - 1, 1), (rows - 1, 2))


def local_kernel(
    choice_ref, x_ref, edge_ref, narrow_ref, down_ref, up_ref, x_out, narrow_out, ext
):
    rows = narrow_ref.shape[0]
    edges = edge_blocks(rows)
    none = jnp.zeros((BS, BS), jnp.bfloat16)
    for r in (0, 1, rows + 2, rows + 3):
        for q in range(3):
            ext[r, q] = none
    for r in range(rows):
        for q in range(3):
            if (r, q) in edges:
                place = edges.index((r, q))
                ext[r + 2, q] = down_ref[place] if place < 3 else up_ref[place - 3]
            else:
                ext[r + 2, q] = narrow_ref[r, q]
    twice = choice_ref[0] == 1

    @pl.loop(0, rows)
    def _(row):
        i = row + 2
        here = [ext[i, q] for q in range(3)]
        up1, up0 = ext[i - 1, 1], ext[i - 1, 2]
        upup = ext[i - 2, 2]
        dn1, dn0 = ext[i + 1, 1], ext[i + 1, 0]
        dd = ext[i + 2, 0]
        diag = (
            dot32(here[0], here[0], NT)
            + dot32(here[1], here[1], NT)
            + dot32(here[2], here[2], NT)
            + dot32(dn1, dn1, TN)
            + dot32(dd, dd, TN)
        )
        near = (
            dot32(here[0], up1, NT)
            + dot32(here[1], up0, NN)
            + dot32(here[2], here[1], NN)
            + dot32(dn1, dn0, TN)
        )
        far = dot32(here[0], upup, NN) + dot32(here[1], up1, NN) + dot32(here[2], here[0], NN)
        for q, squared in ((0, far), (1, near), (2, diag)):
            new = jnp.where(twice, 2.0 * x_ref[row, q] - squared, squared)
            x_out[row, q] = new
            narrow_out[row, q] = new.astype(jnp.bfloat16)

    @pl.when(twice)
    def _():
        for place, (r, q) in enumerate(edges):
            x_out[r, q] += 2.0 * (edge_ref[place] - x_ref[r, q])


def local_step(choice, x, edge, narrow, down, up):
    rows = x.shape[0]
    vmem = pl.BlockSpec(memory_space=pltpu.VMEM)
    return pl.pallas_call(
        local_kernel,
        in_specs=[pl.BlockSpec(memory_space=pltpu.SMEM)] + [vmem] * 5,
        out_specs=[vmem, vmem],
        out_shape=[
            jax.ShapeDtypeStruct(x.shape, jnp.float32),
            jax.ShapeDtypeStruct(x.shape, jnp.bfloat16),
        ],
        scratch_shapes=[pltpu.VMEM((rows + 4, 3, BS, BS), jnp.bfloat16)],
        compiler_params=pltpu.CompilerParams(vmem_limit_bytes=8 << 20),
        cost_estimate=pl.CostEstimate(
            flops=rows * 12 * 2 * BS**3, bytes_accessed=x.size * 4, transcendentals=0
        ),
        name="local_step",
    )(choice, x, edge, narrow, down, up)


def border_kernel(
    choice_ref, before_ref, top_ref, bottom_ref, x_ref, edge_out, down_out, up_out
):
    rows = x_ref.shape[0]
    sign = jnp.where(choice_ref[0] == 1, -1.0, 1.0)
    x00, x01, x10 = before_ref[0], before_ref[1], before_ref[2]
    t_far, t_mid, t_near = top_ref[0], top_ref[1], top_ref[2]
    b_far, b_near, b_last = bottom_ref[0], bottom_ref[1], bottom_ref[2]
    added = (
        lambda: dot32(x00, t_far, NN) + dot32(x01, t_mid, NN),
        lambda: dot32(x00, t_mid, NT) + dot32(x01, t_near, NN),
        lambda: dot32(x10, t_near, NN),
        lambda: dot32(b_far, b_far, TN),
        lambda: dot32(b_near, b_far, TN),
        lambda: dot32(b_near, b_near, TN) + dot32(b_last, b_last, TN),
    )
    for place, (r, q) in enumerate(edge_blocks(rows)):
        new = x_ref[r, q] + sign * added[place]()
        edge_out[place] = new
        if place < 3:
            down_out[place] = new.astype(jnp.bfloat16)
        else:
            up_out[place - 3] = new.astype(jnp.bfloat16)


def border_step(choice, before, top, bottom, x):
    vmem = pl.BlockSpec(memory_space=pltpu.VMEM)
    edge = jax.ShapeDtypeStruct(top.shape, jnp.bfloat16)
    return pl.pallas_call(
        border_kernel,
        in_specs=[pl.BlockSpec(memory_space=pltpu.SMEM)] + [vmem] * 4,
        out_specs=[vmem] * 3,
        out_shape=[jax.ShapeDtypeStruct((6, BS, BS), jnp.float32), edge, edge],
        compiler_params=pltpu.CompilerParams(vmem_limit_bytes=4 << 20),
        cost_estimate=pl.CostEstimate(
            flops=9 * 2 * BS**3, bytes_accessed=x.size, transcendentals=0
        ),
        name="border_step",
    )(choice, before, top, bottom, x)


def density_kernel(x_ref, edge_ref, out, sems):
    rows = x_ref.shape[0]
    edges = edge_blocks(rows)
    copies = []
    for r in range(rows):
        for q in range(3):
            source = edge_ref.at[edges.index((r, q))] if (r, q) in edges else x_ref.at[r, q]
            copies.append(pltpu.make_async_copy(source, out.at[r, q], sems.at[r * 3 + q]))
    for copy in copies:
        copy.start()
    for copy in copies:
        copy.wait()


def density_step(x, edge):
    vmem = pl.BlockSpec(memory_space=pltpu.VMEM)
    return pl.pallas_call(
        density_kernel,
        in_specs=[vmem, vmem],
        out_specs=pl.BlockSpec(memory_space=pltpu.HBM),
        out_shape=pltpu.HBM(x.shape, jnp.float32),
        scratch_shapes=[pltpu.SemaphoreType.DMA((x.shape[0] * 3,))],
        compiler_params=pltpu.CompilerParams(vmem_limit_bytes=8 << 20),
        cost_estimate=pl.CostEstimate(flops=0, bytes_accessed=x.size * 4, transcendentals=0),
        name="density_step",
    )(x, edge)


def plan_kernel(moves, geometry, blocks_ref, basis_ref, *refs):
    *outs, table_ref, buf, in_sems, out_sems = refs
    rows, band_count, grid_count = geometry
    local = basis_ref.shape[0]
    band = lax.axis_index("band")
    grid = lax.axis_index("grid")
    device = band * grid_count + grid
    own_moves = []
    for d in range(local):
        first = blocks_ref[0, device * local + d]
        own_moves.append(first // (rows * grid_count) - band)

    def place_of(move):
        place = jnp.int32(0)
        for d in range(local):
            place = jnp.where(own_moves[d] == move, d, place)
        return place

    for n, move in enumerate(moves):
        pltpu.make_async_copy(basis_ref.at[place_of(move)], buf.at[n], in_sems.at[n]).start()
    table_ref[OWN_PLACE] = place_of(0)
    for slot, move in enumerate(SLOT_MOVES):
        source = band - move
        live = (source >= 0) & (source < band_count)
        source = jnp.clip(source, 0, band_count - 1) * grid_count + grid
        start = jnp.int32(0)
        count = jnp.int32(0)
        for d in range(local):
            first = blocks_ref[0, source * local + d]
            match = live & (first // rows == device)
            blocks = jnp.int32(0)
            for k in range(DBLK):
                blocks += jnp.where(blocks_ref[k, source * local + d] >= 0, 1, 0)
            start = jnp.where(match, first - device * rows, start)
            count = jnp.where(match, blocks, count)
        table_ref[STARTS + slot] = start
        table_ref[COUNTS + slot] = count
    for d in range(local):
        table_ref[MOVES + d] = own_moves[d]
    for n, move in enumerate(moves):
        pltpu.make_async_copy(basis_ref.at[place_of(move)], buf.at[n], in_sems.at[n]).wait()
        pltpu.make_async_copy(buf.at[n], outs[n], out_sems.at[n]).start()
    for n, move in enumerate(moves):
        pltpu.make_async_copy(buf.at[n], outs[n], out_sems.at[n]).wait()


def plan_step(moves, blocks, basis, rows, band_count, grid_count):
    any_space = pl.BlockSpec(memory_space=pl.ANY)
    smem = pl.BlockSpec(memory_space=pltpu.SMEM)
    one = jax.ShapeDtypeStruct(basis.shape[1:], basis.dtype)
    return pl.pallas_call(
        functools.partial(plan_kernel, moves, (rows, band_count, grid_count)),
        in_specs=[smem, pl.BlockSpec(memory_space=pltpu.HBM)],
        out_specs=[any_space] * len(moves) + [smem],
        out_shape=[one] * len(moves) + [jax.ShapeDtypeStruct((TABLE,), jnp.int32)],
        scratch_shapes=[
            pltpu.VMEM((len(moves),) + basis.shape[1:], basis.dtype),
            pltpu.SemaphoreType.DMA((len(moves),)),
            pltpu.SemaphoreType.DMA((len(moves),)),
        ],
        compiler_params=pltpu.CompilerParams(vmem_limit_bytes=16 << 20),
        name="plan_step",
    )(blocks, basis)


def pick_kernel(moves, cuts, table_ref, basis_ref, *refs):
    *outs, buf, in_sems, out_sems = refs
    local = basis_ref.shape[0]

    def place_of(move):
        place = jnp.int32(0)
        for d in range(local):
            place = jnp.where(table_ref[MOVES + d] == move, d, place)
        return place

    def load(n):
        return pltpu.make_async_copy(basis_ref.at[place_of(moves[n])], buf.at[n], in_sems.at[n])

    def stores(n):
        return [
            pltpu.make_async_copy(
                buf.at[n, pl.ds(low, high - low)],
                outs[n * len(cuts) + c],
                out_sems.at[n * len(cuts) + c],
            )
            for c, (low, high) in enumerate(cuts)
        ]

    for n in range(len(moves)):
        load(n).start()
    for n in range(len(moves)):
        load(n).wait()
        for copy in stores(n):
            copy.start()
    for n in range(len(moves)):
        for copy in stores(n):
            copy.wait()


def pick_step(moves, cuts, table, basis):
    any_space = pl.BlockSpec(memory_space=pl.ANY)
    smem = pl.BlockSpec(memory_space=pltpu.SMEM)
    width = basis.shape[2]
    outs = [jax.ShapeDtypeStruct((high - low, width), basis.dtype) for low, high in cuts]
    return pl.pallas_call(
        functools.partial(pick_kernel, moves, cuts),
        in_specs=[smem, pl.BlockSpec(memory_space=pltpu.HBM)],
        out_specs=[any_space] * (len(moves) * len(cuts)),
        out_shape=outs * len(moves),
        scratch_shapes=[
            pltpu.VMEM((len(moves),) + basis.shape[1:], basis.dtype),
            pltpu.SemaphoreType.DMA((len(moves),)),
            pltpu.SemaphoreType.DMA((len(moves) * len(cuts),)),
        ],
        compiler_params=pltpu.CompilerParams(vmem_limit_bytes=16 << 20),
        name="pick_step",
    )(table, basis)


def fill_stack(tile_refs, stack):
    main, down, up = tile_refs
    rows = main.shape[0]
    edges = edge_blocks(rows)

    def tile(r, q):
        if (r, q) not in edges:
            return main[r, q]
        place = edges.index((r, q))
        return down[place] if place < 3 else up[place - 3]

    for r in range(rows):
        stack[r, 0:BS] = tile(r, 2)
        for gap in (1, 2):
            where = pl.ds(gap * BS, BS)
            if r + gap < rows:
                stack[r, where] = tile(r + gap, 2 - gap) * 2
            else:
                stack[r, where] = jnp.zeros((BS, BS), jnp.bfloat16)


def blank_tail(phi, slot, blocks):
    for k in range(2, DBLK):

        @pl.when(k >= blocks)
        def _():
            phi[slot, :, k * BS : (k + 1) * BS] = jnp.zeros((phi.shape[1], BS), jnp.bfloat16)


def potential_of_slot(phi, slot, first, stack, pot_out, psi_at, factor):
    points = phi.shape[1]
    rows = stack.shape[0]

    @pl.loop(0, points // TILE)
    def _(step):
        here = pl.ds(pl.multiple_of(step * TILE, TILE), TILE)
        total = jnp.zeros((TILE, BS), jnp.float32)
        for j in range(DBLK):
            last = min(j + 3, DBLK)
            row = jnp.minimum(first + j, rows - 1)
            applied = dot32(phi[slot, here, j * BS : last * BS], stack[row, 0 : (last - j) * BS], NN)
            total += applied * phi[slot, here, j * BS : (j + 1) * BS].astype(jnp.float32)
        potential = jnp.tanh(jnp.sum(total, axis=1, keepdims=True))
        spread = jnp.transpose(jnp.broadcast_to(potential, (TILE, 128)))
        pot_out[slot, :, here] = spread[0:1]
        scale = factor * potential
        psi_at(here)[...] = (scale * phi[slot, here, :].astype(jnp.float32)).astype(jnp.bfloat16)


def add_blocks(ham, psi, phi, slot, first):
    for k in range(DBLK):
        row = jnp.minimum(first + k, ham.shape[0] - 1)
        low = max(0, k - 2)
        piece = dot32(psi[:, k * BS : (k + 1) * BS], phi[slot, :, low * BS : (k + 1) * BS], TN)
        for j in range(low, k + 1):
            ham[row, 2 - (k - j)] += piece[:, (j - low) * BS : (j - low + 1) * BS]


def domain_kernel(slots, factor, table_ref, *refs):
    refs = list(refs)
    tile_refs = [refs.pop(0) for _ in range(3)]
    basis_refs = [refs.pop(0) for _ in slots]
    ham, pot_out, stack, phi, psi, sems = refs

    def fetch(n):
        source = basis_refs[n]
        if len(source.shape) == 3:
            source = source.at[table_ref[OWN_PLACE]]
        return pltpu.make_async_copy(source, phi.at[n], sems.at[n])

    for n in range(len(slots)):
        fetch(n).start()
    for r in range(ham.shape[0]):
        ham[r] = jnp.zeros_like(ham[r])
    fill_stack(tile_refs, stack)
    pot_out[...] = jnp.zeros_like(pot_out)
    for n in range(len(slots)):
        fetch(n).wait()

    @pl.loop(0, len(slots))
    def _(n):
        first = table_ref[STARTS + slots[0] + n]
        blocks = table_ref[COUNTS + slots[0] + n]

        @pl.when(blocks > 0)
        def _():
            blank_tail(phi, n, blocks)
            potential_of_slot(phi, n, first, stack, pot_out, lambda here: psi.at[here], factor)
            add_blocks(ham, psi, phi, n, first)


def domain_step(slots, table, tiles, arrays, factor):
    rows = RB
    points, width = arrays[-1].shape[-2:]
    number = len(arrays)
    smem = pl.BlockSpec(memory_space=pltpu.SMEM)
    vmem = pl.BlockSpec(memory_space=pltpu.VMEM)
    hbm = pl.BlockSpec(memory_space=pl.ANY)
    outs = [
        jax.ShapeDtypeStruct((rows, 3, BS, BS), jnp.float32),
        jax.ShapeDtypeStruct((number, 1, points), jnp.float32),
        jax.ShapeDtypeStruct((rows, 3 * BS, BS), jnp.bfloat16),
    ]
    return pl.pallas_call(
        functools.partial(domain_kernel, slots, factor),
        in_specs=[smem] + [vmem] * len(tiles) + [hbm] * number,
        out_specs=[vmem] * len(outs),
        out_shape=outs,
        scratch_shapes=[
            pltpu.VMEM((number, points, width), jnp.bfloat16),
            pltpu.VMEM((points, width), jnp.bfloat16),
            pltpu.SemaphoreType.DMA((number,)),
        ],
        compiler_params=pltpu.CompilerParams(
            vmem_limit_bytes=(8 << 20) + number * points * width * 2
        ),
        cost_estimate=pl.CostEstimate(
            flops=number * 24 * 2 * points * BS * BS,
            bytes_accessed=number * points * width * 2 + rows * 3 * BS * BS * 6,
            transcendentals=number * points,
        ),
        name="domain_step",
    )(table, *tiles, *arrays)


def potential_kernel(slots, factor, table_ref, stack, *refs):
    *given, psi_out, phi_out, pot_out, phi = refs
    basis_refs, detour_refs = given[: len(slots)], given[len(slots) :]
    points, width = phi.shape[1:]
    pad = phi_out.shape[2] - width
    grid = lax.axis_index("grid")
    last = lax.axis_size("grid") - 1
    detoured = (grid <= 1, grid >= last - 1)
    pot_out[...] = jnp.zeros_like(pot_out)
    for n in range(len(slots)):
        phi[n] = basis_refs[n][...]
        for detour_ref in detour_refs:

            @pl.when(detoured[n])
            def _():
                phi[n] = detour_ref[...]

        phi_out[n, :, 0:pad] = jnp.zeros((points, pad), jnp.bfloat16)
        phi_out[n, :, pad:] = phi[n]
        psi_out[n, :, width:] = jnp.zeros((points, BS), jnp.bfloat16)

    @pl.loop(0, len(slots))
    def _(n):
        first = table_ref[STARTS + slots[0] + n]
        blocks = table_ref[COUNTS + slots[0] + n]

        @pl.when(blocks > 0)
        def _():
            blank_tail(phi, n, blocks)

            def psi_at(here):
                return psi_out.at[n, here, 0:width]

            potential_of_slot(phi, n, first, stack, pot_out, psi_at, factor)


def potential_step(slots, table, stack, arrays, detours, factor):
    points, width = arrays[-1].shape
    number = len(arrays)
    smem = pl.BlockSpec(memory_space=pltpu.SMEM)
    vmem = pl.BlockSpec(memory_space=pltpu.VMEM)
    return pl.pallas_call(
        functools.partial(potential_kernel, slots, factor),
        in_specs=[smem] + [vmem] * (1 + number + len(detours)),
        out_specs=[vmem] * 3,
        out_shape=[
            jax.ShapeDtypeStruct((number, points, width + BS), jnp.bfloat16),
            jax.ShapeDtypeStruct((number, points, width + 2 * BS), jnp.bfloat16),
            jax.ShapeDtypeStruct((number, 1, points), jnp.float32),
        ],
        scratch_shapes=[pltpu.VMEM((number, points, width), jnp.bfloat16)],
        compiler_params=pltpu.CompilerParams(vmem_limit_bytes=12 << 20),
        cost_estimate=pl.CostEstimate(
            flops=number * 12 * 2 * points * BS * BS,
            bytes_accessed=number * points * width * 4,
            transcendentals=number * points,
        ),
        name="potential_step",
    )(table, stack, *arrays, *detours)


def block_kernel(slots, table_ref, base_ref, *refs):
    *parts, ham_out, ham, sems = refs
    rows = ham.shape[0]

    def send(r):
        return pltpu.make_async_copy(ham.at[r], ham_out.at[r], sems.at[r])

    for r in range(rows):
        total = None
        for n, slot in enumerate(slots):
            k = r - table_ref[STARTS + slot]
            held = (k >= 0) & (k < table_ref[COUNTS + slot])
            near = jnp.clip(k, 0, DBLK - 1)
            left = pl.ds(pl.multiple_of(jnp.where(held, near, DBLK) * BS, BS), BS)
            right = pl.ds(pl.multiple_of(near * BS, BS), 3 * BS)
            for psi_ref, phi_ref in zip(parts[::2], parts[1::2]):
                piece = dot32(psi_ref[n, :, left], phi_ref[n, :, right], TN)
                total = piece if total is None else total + piece
        for q in range(3):
            ham[r, q] = base_ref[r, q] + total[:, q * BS : (q + 1) * BS]
        send(r).start()
    for r in range(rows):
        send(r).wait()


def block_step(slots, table, base, parts):
    rows = base.shape[0]
    size = sum(part.size for part in parts)
    smem = pl.BlockSpec(memory_space=pltpu.SMEM)
    vmem = pl.BlockSpec(memory_space=pltpu.VMEM)
    return pl.pallas_call(
        functools.partial(block_kernel, slots),
        in_specs=[smem, vmem] + [vmem] * len(parts),
        out_specs=pl.BlockSpec(memory_space=pltpu.HBM),
        out_shape=pltpu.HBM(base.shape, jnp.float32),
        scratch_shapes=[
            pltpu.VMEM(base.shape, jnp.float32),
            pltpu.SemaphoreType.DMA((rows,)),
        ],
        compiler_params=pltpu.CompilerParams(vmem_limit_bytes=10 << 20),
        cost_estimate=pl.CostEstimate(
            flops=size * 3 * BS,
            bytes_accessed=size * 2 + base.size * 8,
            transcendentals=0,
        ),
        name="block_step",
    )(table, base, *parts)


def whole_step(x_initial, sp2_choices, domain_blocks, basis_values):
    row_count = x_initial.shape[0]
    band_count = lax.axis_size("band")
    grid_count = lax.axis_size("grid")
    local_domains, points, width = basis_values.shape
    factor = width / points
    cuts = ((0, 512), (512, points))

    def orbitals(value, move):
        return passed_along(value, "band", move)

    basis_values = pltpu.with_memory_space_constraint(basis_values, pltpu.HBM)
    blocks = pltpu.with_memory_space_constraint(domain_blocks.T, pltpu.HBM)
    plus, minus, table = plan_step(
        (2, -2), blocks, basis_values, row_count, band_count, grid_count
    )
    halfway = [orbitals(plus, 1), orbitals(minus, -1)]
    plus, minus = pick_step((1, -1), ((0, points),), table, basis_values)
    near = [orbitals(plus, 1), orbitals(minus, -1)]
    far_a = [orbitals(halfway[n][: cuts[0][1]], 1 - 2 * n) for n in (0, 1)]
    rest = [halfway[n][cuts[1][0] :] for n in (0, 1)]
    turned = jnp.where(lax.axis_index("grid") < grid_count // 2, rest[0], rest[1])
    detour = lax.ppermute(turned, ("band", "grid"), detour_out(band_count, grid_count))
    far_b = []
    for n, skipped in ((0, (0, 1)), (1, (grid_count - 2, grid_count - 1))):
        move = 1 - 2 * n
        pairs = [
            (b * grid_count + g, (b + move) * grid_count + g)
            for b in range(band_count)
            for g in range(grid_count)
            if 0 <= b + move < band_count and g not in skipped
        ]
        far_b.append(lax.ppermute(rest[n], ("band", "grid"), pairs))
    detour = lax.ppermute(detour, ("band", "grid"), detour_back(band_count, grid_count))

    x = x_initial
    narrow = x.astype(jnp.bfloat16)
    upward = jnp.stack([narrow[-2, 2], narrow[-1, 1], narrow[-1, 2]])
    downward = jnp.stack([narrow[0, 0], narrow[0, 1], narrow[1, 0]])
    edge = jnp.stack([x[r, q] for r, q in edge_blocks(row_count)])
    for iteration in range(ITERS):
        choice = sp2_choices[iteration : iteration + 1]
        top = passed_along(upward, ("band", "grid"), 1)
        bottom = passed_along(downward, ("band", "grid"), -1)
        before = downward
        x, narrow = local_step(choice, x, edge, narrow, downward, upward)
        edge, downward, upward = border_step(choice, before, top, bottom, x)
    tiles = (narrow, downward, upward)
    density = density_step(x, edge)

    ham, near_pot, stack = domain_step(
        (0, 1, 2), table, tiles, [basis_values] + near, factor
    )
    psi_a, phi_a, pot_a = potential_step((3, 4), table, stack, far_a, [], factor)
    psi_b, phi_b, pot_b = potential_step((3, 4), table, stack, far_b, [detour], factor)
    far_pot = [jnp.concatenate([pot_a[n, 0], pot_b[n, 0]]) for n in (0, 1)]
    ham = block_step((3, 4), table, ham, [psi_a, phi_a, psi_b, phi_b])
    sent_back = [near_pot[0, 0]]
    for move, values in ((1, near_pot[1, 0]), (-1, near_pot[2, 0]), (2, far_pot[0]), (-2, far_pot[1])):
        sent_back.append(passed_along(values, "band", -move))
    own_moves = table[MOVES : MOVES + local_domains]
    own_potential = jnp.zeros((local_domains, points), jnp.float32)
    for move, values in zip(SLOT_MOVES, sent_back):
        own_potential = jnp.where((own_moves == move)[:, None], values[None, :], own_potential)
    return density, ham, own_potential


def solution(mesh):
    placed = (P(("band", "grid"), None, None, None), P(), P(), P(("band", "grid"), None, None))
    return jax.shard_map(
        whole_step,
        mesh=mesh,
        in_specs=placed,
        out_specs=(
            P(("band", "grid"), None, None, None),
            P(("band", "grid"), None, None, None),
            P(("band", "grid"), None),
        ),
        check_vma=False,
    )
```
